512 devices in a mesh: ctx: 64 (over x, z, core), head: 8 (over y).
Axes of the slice: x: 4, y: 8, z: 8, core: 2. Of those that a mesh axis runs over, the one named last changes fastest.
Arguments:
- lin_query: bfloat16 [8192, 8192], P('ctx', 'head'), may hold values from -6 to 6
- lin_key: bfloat16 [8192, 8192], P('ctx', 'head'), may hold values from -0.5 to 0.5
- lin_value: bfloat16 [8192, 8192], P('ctx', 'head'), may hold values from -9 to 9
- log_decay: float32 [64, 8192], P('head', 'ctx'), may hold values from -0.75 to 0
- norm_gain: float32 [8192], P('head'), may hold values from 0.1 to 1.9
- soft_query: bfloat16 [8192, 8192], P('ctx', 'head'), may hold values from -8 to 8
- soft_key: bfloat16 [8192, 1024], P('ctx', 'head'), may hold values from -8 to 8
- soft_value: bfloat16 [8192, 1024], P('ctx', 'head'), may hold values from -6 to 6
- doc_lengths: int32 [32], replicated, may hold values from 1 to 1024, 8192 in all
Outputs:
- lightning_out: bfloat16 [8192, 8192], P('ctx', 'head')
- softmax_out: bfloat16 [8192, 8192], P('ctx', 'head')
The draws below stay inside these ranges and needn't reach their ends.
Inputs may be any that keep to these rules, and one draw needn't show every extreme that they name: `doc_lengths`: the lengths sum to 8192; the largest is exactly 1024.
All inputs are finite; a program needn't handle non-finite values.
Results may differ from the reference program's by a relative error of at most 0.013.
Values may be sent and summed in bfloat16 or wider, within the bound.
A program may use at most 128 MiB of HBM per device.

```python
import math
import jax
import jax.numpy as jnp
import numpy as np
from jax import lax

TOK_DEV = 128
HEADS = 64
KV_HEADS = 8
DH = 128
DOC_SPAN = 8
PACKED_TOKENS = 8192
MAXDOC = 1024
DOCS = 32


def draw_log_decay(key, part):
    random_subkeys = jax.random.split(jax.random.fold_in(key, 11), 6)
    fast_heads = jax.random.randint(random_subkeys[0], (HEADS,), 0, 2) == 0
    fast_rate = jnp.exp(jax.random.uniform(random_subkeys[1], (HEADS,), minval=math.log(1.0 / 50.0), maxval=math.log(1.0 / 30.0)))
    slow_rate = jnp.exp(jax.random.uniform(random_subkeys[2], (HEADS,), minval=math.log(0.1), maxval=0.0)) * (0.5 * math.log(10.0) / MAXDOC)
    head_rate = jnp.where(fast_heads, fast_rate, slow_rate)
    roughness = jax.random.uniform(random_subkeys[3], (HEADS, PACKED_TOKENS), minval=0.5, maxval=1.5)
    value_vectors = -head_rate[:, None] * roughness
    spike_locations = jax.random.randint(random_subkeys[4], (6,), 0, PACKED_TOKENS)
    spike_present = jnp.any(jnp.arange(PACKED_TOKENS)[:, None] == spike_locations[None, :], axis=1)
    spike_penalty = jnp.log(jax.random.uniform(random_subkeys[5], (PACKED_TOKENS,), minval=0.5, maxval=0.8))
    return (value_vectors + jnp.where(spike_present, spike_penalty, 0.0)[None, :]).astype(jnp.float32)


def draw_lin_value(key, part):
    subkey = jax.random.fold_in(key, 23)
    head_number = (jnp.arange(HEADS * DH) // DH).astype(jnp.float32)
    head_ramp = 3.0 ** (head_number / max(HEADS - 1, 1))
    normal_part = jnp.clip(jax.random.normal(subkey, (PACKED_TOKENS, HEADS * DH)), -6.0, 6.0)
    return (normal_part * head_ramp[None, :] * 0.5).astype(jnp.bfloat16)


def softmax_pair(key):
    random_subkeys = jax.random.split(jax.random.fold_in(key, 37), 2)
    group_size = HEADS // KV_HEADS
    query_draw = jnp.clip(jax.random.normal(random_subkeys[0], (PACKED_TOKENS, KV_HEADS, group_size, DH)), -6.0, 6.0)
    key_draw = jnp.clip(jax.random.normal(random_subkeys[1], (PACKED_TOKENS, KV_HEADS, DH)), -6.0, 6.0)
    return (query_draw.reshape(PACKED_TOKENS, HEADS * DH), key_draw.reshape(PACKED_TOKENS, KV_HEADS * DH))


def draw_soft_query(key, part):
    return softmax_pair(key)[0].astype(jnp.bfloat16)


def draw_soft_key(key, part):
    return softmax_pair(key)[1].astype(jnp.bfloat16)


def levels(key, dims, cuts, low, largest):
    level = 1.0
    for position, shards_of in cuts:
        draws = jax.random.uniform(jax.random.fold_in(jax.random.fold_in(key, 6), position), (shards_of,), jnp.float32, low / len(cuts), largest / len(cuts))
        level = level * jnp.repeat(jnp.exp(draws), dims[position] // shards_of).reshape((-1,) + (1,) * (len(dims) - 1 - position))
    return level


def profile(amount, total, most, slope):
    portions = [(1 << 20) // math.isqrt(rank ** slope) + 1 for rank in range(2, amount + 1)]
    spare, counts = total - most - (amount - 1), [1] * (amount - 1)
    while spare > 0:
        candidates = [i for i in range(amount - 1) if counts[i] < most]
        whole, budget = sum([portions[i] for i in candidates]), spare
        for i in candidates:
            addition = min(most - counts[i], max(1, budget * portions[i] // whole), spare)
            counts[i] = counts[i] + addition
            spare = spare - addition
    return np.array([most] + counts)


def uneven(own_key, count, total, limit, skew):
    if count == 2:
        one = jax.random.randint(own_key, (), max(1, total - limit), min(limit, total - 1) + 1)
        return jnp.stack([one, total - one])
    lengths = jnp.asarray(profile(count, total, limit, skew), jnp.int32)
    pairs = (count - 1) // 2
    giver, taker = lengths[1:1 + 2 * pairs:2], lengths[2:2 + 2 * pairs:2]
    room = jnp.minimum(giver - 1, limit - taker)
    moved = jax.random.randint(jax.random.fold_in(own_key, 1), (pairs,), 0, 1 << 20) % (room + 1)
    lengths = lengths.at[1:1 + 2 * pairs:2].set(giver - moved).at[2:2 + 2 * pairs:2].set(taker + moved)
    return lengths[jax.random.permutation(jax.random.fold_in(own_key, 2), count)]


def noise(key, shape, deviation, bound, cuts=(), held_as=jnp.bfloat16):
    array = deviation * jax.random.normal(key, shape, jnp.float32)
    if cuts:
        array = array * levels(key, shape, cuts, -0.22, 0.18)
    return jnp.clip(array, -bound, bound).astype(held_as)


def setup_inputs(seed: int = 0) -> dict:
    arg_keys = jax.random.split(jax.random.key(seed), 10)
    lin_query = noise(arg_keys[0], (PACKED_TOKENS, HEADS * DH), 1.0, 6.0, ((0, 64), (1, 8)))
    lin_key = noise(arg_keys[1], (PACKED_TOKENS, HEADS * DH), DH ** -0.5, 0.5, ((0, 64), (1, 8)))
    lin_value = draw_lin_value(jax.random.fold_in(arg_keys[9], 71), 0)
    log_decay = draw_log_decay(jax.random.fold_in(arg_keys[9], 71), 0)
    norm_gain = jnp.clip(1.0 + 0.18 * jax.random.normal(arg_keys[4], (HEADS * DH,), jnp.float32), 0.1, 1.9)
    soft_query = draw_soft_query(jax.random.fold_in(arg_keys[9], 71), 0)
    soft_key = draw_soft_key(jax.random.fold_in(arg_keys[9], 71), 0)
    soft_value = noise(arg_keys[7], (PACKED_TOKENS, KV_HEADS * DH), 1.0, 6.0, ((0, 64), (1, 8)))
    doc_lengths = uneven(arg_keys[8], DOCS, PACKED_TOKENS, MAXDOC, 2).astype(jnp.int32)
    return dict(lin_query=lin_query, lin_key=lin_key, lin_value=lin_value, log_decay=log_decay, norm_gain=norm_gain, soft_query=soft_query, soft_key=soft_key, soft_value=soft_value, doc_lengths=doc_lengths)


NEG_FILL = -1e+30

def doc_starts(doc_lengths):
    ends = jnp.cumsum(doc_lengths).astype(jnp.int32)
    return (ends - doc_lengths).astype(jnp.int32)

def doc_of(positions, start_offsets):
    hits = (start_offsets[None, :] <= positions[:, None]).astype(jnp.int32)
    return (lax.optimization_barrier(jnp.sum(hits, axis=1)) - 1).astype(jnp.int32)

def stretch_terms(query, key_rows, value_rows, decay_rates, positions, start_offsets):
    log_sum = jnp.cumsum(decay_rates, axis=1)
    doc_ids = doc_of(positions, start_offsets)
    first_pos = positions[0]
    last_pos = positions[-1]
    allowed = (doc_ids[:, None] == doc_ids[None, :]) & (positions[:, None] >= positions[None, :])
    gaps = jnp.where(allowed[None], log_sum[:, :, None] - log_sum[:, None, :], -jnp.inf)
    scores = jnp.einsum('thd,shd->hts', query.astype(jnp.float32), key_rows.astype(jnp.float32))
    weights = lax.optimization_barrier((scores * jnp.exp(gaps)).astype(jnp.bfloat16)).astype(jnp.float32)
    local_part = jnp.einsum('hts,shd->thd', weights, value_rows.astype(jnp.float32))
    in_last_doc = (doc_ids == doc_ids[-1]).astype(jnp.float32)
    key_scale = jnp.exp(log_sum[:, -1:] - log_sum) * in_last_doc[None, :]
    scaled_keys = (key_rows.astype(jnp.float32) * key_scale.T[:, :, None]).astype(jnp.bfloat16)
    scaled_keys = lax.optimization_barrier(scaled_keys).astype(jnp.float32)
    update = jnp.einsum('thd,the->hde', scaled_keys, value_rows.astype(jnp.float32))
    inside = (start_offsets >= first_pos) & (start_offsets <= last_pos)
    factor = jnp.where(jnp.any(inside), 0.0, jnp.exp(log_sum[:, -1]))
    restarted = lax.optimization_barrier(jnp.sum(((start_offsets[None, :] >= first_pos) & (start_offsets[None, :] <= positions[:, None])).astype(jnp.int32), axis=1))
    carried = (restarted == 0).astype(jnp.float32)
    query_scale = jnp.exp(log_sum) * carried[None, :]
    scaled_query = query.astype(jnp.float32) * query_scale.T[:, :, None]
    return (local_part, scaled_query, update, factor)

def lightning_layer(lin_query, lin_key, lin_value, log_decay, norm_gain, start_offsets):
    blocks = PACKED_TOKENS // TOK_DEV
    shape4 = (blocks, TOK_DEV, HEADS, DH)
    rates = log_decay.reshape(HEADS, blocks, TOK_DEV).transpose(1, 0, 2)
    indices = jnp.arange(blocks, dtype=jnp.int32)

    def advance(carried_state, inputs):
        query, key_rows, value_rows, decay_rates, block_index = inputs
        positions = (block_index * TOK_DEV + jnp.arange(TOK_DEV, dtype=jnp.int32)).astype(jnp.int32)
        local_part, scaled_query, update, factor = stretch_terms(query, key_rows, value_rows, decay_rates, positions, start_offsets)
        carried_part = jnp.einsum('thd,hde->the', scaled_query, carried_state, precision=lax.Precision.HIGHEST)
        following = carried_state * factor[:, None, None] + update
        return (following, local_part + carried_part)
    _, mixed = lax.scan(advance, jnp.zeros((HEADS, DH, DH), jnp.float32), (lin_query.reshape(shape4), lin_key.reshape(shape4), lin_value.reshape(shape4), rates, indices))
    mixed = mixed.reshape(PACKED_TOKENS, HEADS * DH)
    mean_square = lax.optimization_barrier(jnp.mean(mixed * mixed, axis=1, keepdims=True))
    return (mixed * lax.rsqrt(mean_square + 1e-05) * norm_gain[None, :]).astype(jnp.bfloat16)

def softmax_layer(soft_query, soft_key, soft_value, start_offsets):
    group_size = HEADS // KV_HEADS
    reach = DOC_SPAN * TOK_DEV
    blocks = PACKED_TOKENS // TOK_DEV
    score_scale = 1.0 / math.sqrt(DH)
    queries = soft_query.reshape(blocks, TOK_DEV, KV_HEADS, group_size, DH)
    padding = jnp.zeros((reach, KV_HEADS * DH), soft_key.dtype)
    key_pad = jnp.concatenate([padding, soft_key], axis=0).reshape(-1, KV_HEADS, DH)
    value_pad = jnp.concatenate([padding, soft_value], axis=0).reshape(-1, KV_HEADS, DH)

    def one_block(inputs):
        query_block, block_index = inputs
        begin = (block_index * TOK_DEV).astype(jnp.int32)
        key_rows = lax.dynamic_slice_in_dim(key_pad, begin, reach + TOK_DEV, 0)
        value_rows = lax.dynamic_slice_in_dim(value_pad, begin, reach + TOK_DEV, 0)
        key_pos = (begin - reach + jnp.arange(reach + TOK_DEV, dtype=jnp.int32)).astype(jnp.int32)
        query_pos = (begin + jnp.arange(TOK_DEV, dtype=jnp.int32)).astype(jnp.int32)
        allowed = (doc_of(key_pos, start_offsets)[None, :] == doc_of(query_pos, start_offsets)[:, None]) & (key_pos[None, :] <= query_pos[:, None])
        scores = jnp.einsum('tkgd,skd->kgts', query_block.astype(jnp.float32), key_rows.astype(jnp.float32)) * score_scale
        scores = jnp.where(allowed, scores, NEG_FILL)
        top_score = lax.optimization_barrier(jnp.max(scores, axis=-1))
        probs = jnp.where(allowed, jnp.exp(scores - top_score[..., None]), 0.0)
        total_score = lax.optimization_barrier(jnp.sum(probs, axis=-1))
        rounded = lax.optimization_barrier(probs.astype(jnp.bfloat16)).astype(jnp.float32)
        weighted = jnp.einsum('kgts,skd->kgtd', rounded, value_rows.astype(jnp.float32))
        attended = weighted / total_score[..., None]
        return jnp.transpose(attended, (2, 0, 1, 3)).reshape(TOK_DEV, HEADS * DH)
    outputs = lax.map(one_block, (queries, jnp.arange(blocks, dtype=jnp.int32)))
    return outputs.reshape(PACKED_TOKENS, HEADS * DH).astype(jnp.bfloat16)

def reference(lin_query, lin_key, lin_value, log_decay, norm_gain, soft_query, soft_key, soft_value, doc_lengths):
    start_offsets = doc_starts(doc_lengths)
    lightning_out = lightning_layer(lin_query, lin_key, lin_value, log_decay, norm_gain, start_offsets)
    softmax_out = softmax_layer(soft_query, soft_key, soft_value, start_offsets)
    return (lightning_out, softmax_out)
```

```python
import functools
import math

import jax
import jax.numpy as jnp
from jax import lax
from jax.experimental import pallas as pl
from jax.experimental.pallas import tpu as pltpu
from jax.sharding import PartitionSpec as P

MESH = pl.DeviceIdType.MESH
F32 = jnp.float32
BF16 = jnp.bfloat16
LOG2E = 1.4426950408889634
T = 128
NH = 8
LANE = 4
BLOCK = 4
OFFSET = 2
BACK = 4
NEG = -1e30


def nt(a, b, **kw):
    return lax.dot_general(a, b, (((1,), (1,)), ((), ())), preferred_element_type=F32, **kw)


def mm(a, b, **kw):
    return jnp.dot(a, b, preferred_element_type=F32, **kw)


def rcopy(src, dst, send, recv, dev):
    return pltpu.make_async_remote_copy(
        src_ref=src, dst_ref=dst, send_sem=send, recv_sem=recv, device_id=dev, device_id_type=MESH
    )


def cols(h):
    return pl.ds(pl.multiple_of(h * T, T), T)


def kernel(
    nctx,
    nhead,
    lens,
    lq_hbm,
    lk_hbm,
    lv_hbm,
    ld_ref,
    gain_ref,
    sq_hbm,
    sk_hbm,
    sv_hbm,
    lo_out,
    so_out,
    lq,
    lk,
    lv,
    qs,
    kbuf,
    vbuf,
    bias,
    g_ref,
    ks_ref,
    fown,
    fsib,
    uown,
    usib,
    vst,
    qbuf,
    ebuf,
    y1,
    y2,
    eg,
    mixed,
    yloc,
    ybuf,
    lout,
    sout,
    in_sem,
    kv_s,
    kv_r,
    ks_s,
    ks_r,
    u_s,
    u_r,
    f_s,
    f_r,
    q_s,
    q_r,
    e_r,
    y2_s,
    es_s,
    es_r,
    yy_s,
    yy_r,
    out_sem,
):
    c = lax.axis_index("ctx")
    hd = lax.axis_index("head")
    lane = lax.rem(c, 2)
    chip = lax.div(c, 2)
    role = lax.rem(chip + OFFSET, BLOCK)
    nxt = (lax.rem(c + 2, nctx), hd)
    prv = (lax.rem(c + nctx - 2, nctx), hd)
    sib = (c + 1 - 2 * lane, hd)
    first = c * T

    bar = pltpu.get_barrier_semaphore()
    for dev in (nxt, prv, sib):
        pl.semaphore_signal(bar, inc=1, device_id=dev, device_id_type=MESH)
    for i in range(1, nhead):
        pl.semaphore_signal(
            bar, inc=1, device_id=(c, lax.rem(hd + i, nhead)), device_id_type=MESH
        )

    def slot(i):
        return pl.ds(pl.multiple_of(((BACK - i) * 2 + lane) * T, T), T)

    vc = pl.ds(0, T)
    loads = [
        pltpu.make_async_copy(lk_hbm, lk, in_sem.at[0]),
        pltpu.make_async_copy(lv_hbm, lv, in_sem.at[1]),
        pltpu.make_async_copy(sk_hbm, kbuf.at[slot(0)], in_sem.at[2]),
        pltpu.make_async_copy(sv_hbm, vbuf.at[slot(0), vc], in_sem.at[3]),
        pltpu.make_async_copy(lq_hbm, lq, in_sem.at[4]),
    ]
    for h in range(NH):
        loads.append(
            pltpu.make_async_copy(
                sq_hbm.at[:, pl.ds(h * T, T)], qs.at[pl.ds(h * T, T)], in_sem.at[5 + h]
            )
        )
    for cp in loads:
        cp.start()

    lane_i = lax.broadcasted_iota(jnp.int32, (8, T), 1)
    pos = first + lane_i
    start = jnp.int32(0)
    low = jnp.zeros((8, T), jnp.int32)
    low_end = jnp.int32(0)
    for d in range(lens.shape[0]):
        low = jnp.where(pos >= start, start, low)
        low_end = jnp.where(first + T - 1 >= start, start, low_end)
        start = start + lens[d]
    rel_row = (low - first).astype(F32)
    rel_col = jnp.broadcast_to(rel_row[0:1], (T, T)).T
    row_f = lax.broadcasted_iota(jnp.int32, (T, T), 0).astype(F32)
    col_f = lax.broadcasted_iota(jnp.int32, (T, T), 1).astype(F32)

    tri = jnp.where(row_f <= col_f, 1.0, 0.0)
    both = jnp.concatenate([tri, jnp.ones((T, T), F32)], axis=1)
    sums = mm(ld_ref[...], both, precision=lax.Precision.HIGHEST)
    g = sums[:, :T]
    gend = sums[:, T:]
    g_ref[...] = g
    ks_ref[...] = jnp.where(pos >= low_end, jnp.exp(gend - g), 0.0)
    fown[...] = jnp.where(low_end >= first, 0.0, jnp.exp(gend))

    pl.semaphore_wait(bar, 3 + nhead - 1)

    fcopy = rcopy(fown, fsib, f_s, f_r, sib)
    fcopy.start()

    def kv_next(i):
        return [
            rcopy(kbuf.at[slot(i)], kbuf.at[slot(i + 1)], kv_s.at[i, 0], kv_r.at[i, 0], nxt),
            rcopy(
                vbuf.at[slot(i), vc],
                vbuf.at[slot(i + 1), vc],
                kv_s.at[i, 1],
                kv_r.at[i, 1],
                nxt,
            ),
        ]

    def kv_side(i):
        return [
            rcopy(kbuf.at[slot(i)], kbuf.at[slot(i)], ks_s.at[i, 0], ks_r.at[i, 0], sib),
            rcopy(
                vbuf.at[slot(i), vc], vbuf.at[slot(i), vc], ks_s.at[i, 1], ks_r.at[i, 1], sib
            ),
        ]

    def kv_step(i):
        if i > 0:
            for cp in kv_next(i - 1):
                cp.wait_recv()
        for cp in (kv_next(i) if i < BACK else []) + kv_side(i):
            cp.start()

    loads[2].wait()
    loads[3].wait()
    kv_step(0)

    loads[0].wait()
    loads[1].wait()

    def update(j, _):
        h = lax.rem(j + LANE - LANE * lane, NH)
        kt = lk[:, cols(h)].astype(F32).T
        sk = (kt * ks_ref[pl.ds(h, 1), :]).astype(BF16)
        uown[h] = mm(sk, lv[:, cols(h)]).astype(BF16)
        rcopy(uown.at[h], usib.at[h], u_s.at[h], u_r.at[h], sib).start()
        return 0

    lax.fori_loop(0, NH, update, 0)

    kv_step(1)

    fcopy.wait_recv()
    on_b = lane == 1

    def phase1(j, _):
        h = LANE * lane + j
        rcopy(uown.at[h], usib.at[h], u_s.at[h], u_r.at[h], sib).wait_recv()
        fo = fown[pl.ds(h, 1), :]
        fs = fsib[pl.ds(h, 1), :]
        one = jnp.ones_like(fo)
        a = jnp.where(on_b, one, fs)
        b = jnp.where(on_b, fo, one)
        v = a * uown[h].astype(F32) + b * usib[h].astype(F32)
        vst[j] = v

        @pl.when(role == 0)
        def _():
            y1[j] = v.astype(BF16)

        @pl.when(role > 0)
        def _():
            rcopy(y1.at[j], qbuf.at[j], q_s.at[j], q_r.at[j], nxt).wait_recv()
            y1[j] = (v + (fo * fs) * qbuf[j].astype(F32)).astype(BF16)

        @pl.when(role < BLOCK - 1)
        def _():
            rcopy(y1.at[j], qbuf.at[j], q_s.at[j], q_r.at[j], nxt).start()

        @pl.when(role == BLOCK - 1)
        def _():
            rcopy(y1.at[j], ebuf.at[h], q_s.at[j], e_r.at[j], nxt).start()

        return 0

    lax.fori_loop(0, LANE, phase1, 0)

    own_ok = (col_f >= rel_col) & (col_f <= row_f)
    carried = jnp.where(rel_col < 0.0, 1.0, 0.0)
    loads[4].wait()

    def inside(h, _):
        grow = g_ref[pl.ds(h, 1), :]
        gcol = jnp.broadcast_to(grow, (T, T)).T
        eg[h] = jnp.exp(gcol) * carried
        decay = jnp.exp(jnp.where(own_ok, gcol - grow, NEG))
        w = (nt(lq[:, cols(h)], lk[:, cols(h)]) * decay).astype(BF16)
        mixed[h] = mm(w, lv[:, cols(h)])
        return 0

    lax.fori_loop(0, NH, inside, 0)

    kv_step(2)

    def phase2(j, _):
        h = LANE * lane + j
        rcopy(y2.at[j], ebuf.at[h], y2_s.at[j], e_r.at[j], nxt).wait_recv()

        @pl.when(role < BLOCK - 1)
        def _():
            fo = fown[pl.ds(h, 1), :]
            fs = fsib[pl.ds(h, 1), :]
            y2[j] = (vst[j] + (fo * fs) * ebuf[h].astype(F32)).astype(BF16)
            rcopy(y2.at[j], ebuf.at[h], y2_s.at[j], e_r.at[j], nxt).start()

        rcopy(ebuf.at[h], ebuf.at[h], es_s.at[j], es_r.at[j], sib).start()
        return 0

    lax.fori_loop(0, LANE, phase2, 0)

    def rest(j, _):
        h = LANE * (1 - lane) + j
        rcopy(uown.at[h], usib.at[h], u_s.at[h], u_r.at[h], sib).wait_recv()
        rcopy(ebuf.at[h], ebuf.at[h], es_s.at[j], es_r.at[j], sib).wait_recv()
        return 0

    lax.fori_loop(0, LANE, rest, 0)

    def carry(h, acc):
        fs = fsib[pl.ds(h, 1), :]
        one = jnp.ones_like(fs)
        e1 = jnp.where(on_b, fs, one)
        e2 = jnp.where(on_b, one, jnp.zeros_like(fs))
        s = (e1 * ebuf[h].astype(F32) + e2 * usib[h].astype(F32)).astype(BF16)
        m = mixed[h] + mm(lq[:, cols(h)], s) * eg[h]
        mixed[h] = m
        return acc + m * m

    acc = lax.fori_loop(0, NH, carry, jnp.zeros((T, T), F32))
    part = nt(jnp.ones((8, T), F32), acc, precision=lax.Precision.HIGHEST)
    yloc[...] = part

    def ycopy(i):
        return rcopy(
            yloc, ybuf.at[i], yy_s.at[i], yy_r.at[i], (c, lax.rem(hd + i, nhead))
        )

    for i in range(1, nhead):
        ycopy(i).start()

    kv_step(3)
    kv_step(4)

    for j in range(9):
        rel = col_f + float((j - 8) * T)
        ok = rel >= rel_col
        if j == 8:
            ok = ok & (col_f <= row_f)
        bias[:, pl.ds(j * T, T)] = jnp.where(ok, 0.0, NEG)
    vbuf[:, pl.ds(T, T)] = jnp.ones((vbuf.shape[0], T), BF16)
    for i in range(BACK + 1):
        for cp in kv_side(i):
            cp.wait_recv()
    for cp in loads[5:]:
        cp.wait()
    window = pl.ds(pl.multiple_of(lane * T, T), 9 * T)
    scale2 = LOG2E / math.sqrt(T)

    def attend(h, _):
        s = nt(qs[pl.ds(pl.multiple_of(h * T, T), T), :], kbuf[window, :]) * scale2 + bias[...]
        p = jnp.exp2(s - jnp.max(s, axis=1, keepdims=True)).astype(BF16)
        o = mm(p, vbuf[window, :])
        sout[:, cols(h)] = (o[:, :T] / o[:, T:]).astype(BF16)
        return 0

    lax.fori_loop(0, NH, attend, 0)
    so_copy = pltpu.make_async_copy(sout, so_out, out_sem.at[0])
    so_copy.start()

    total = part
    for i in range(1, nhead):
        ycopy(i).wait_recv()
        total = total + ybuf[i]
    inv_row = lax.rsqrt(total * (1.0 / (nhead * NH * T)) + 1e-05)
    inv = jnp.broadcast_to(inv_row[0:1], (T, T)).T

    def finish(h, _):
        lout[:, cols(h)] = (mixed[h] * inv * gain_ref[pl.ds(h, 1), :]).astype(BF16)
        return 0

    lax.fori_loop(0, NH, finish, 0)
    lo_copy = pltpu.make_async_copy(lout, lo_out, out_sem.at[1])
    lo_copy.start()

    fcopy.wait_send()
    for i in range(BACK + 1):
        for cp in (kv_next(i) if i < BACK else []) + kv_side(i):
            cp.wait_send()

    def sent(h, _):
        rcopy(uown.at[h], usib.at[h], u_s.at[h], u_r.at[h], sib).wait_send()
        return 0

    lax.fori_loop(0, NH, sent, 0)

    def sent2(j, _):
        h = LANE * lane + j
        rcopy(y1.at[j], qbuf.at[j], q_s.at[j], q_r.at[j], nxt).wait_send()
        rcopy(ebuf.at[h], ebuf.at[h], es_s.at[j], es_r.at[j], sib).wait_send()

        @pl.when(role < BLOCK - 1)
        def _():
            rcopy(y2.at[j], ebuf.at[h], y2_s.at[j], e_r.at[j], nxt).wait_send()

        return 0

    lax.fori_loop(0, LANE, sent2, 0)
    for i in range(1, nhead):
        ycopy(i).wait_send()
    so_copy.wait()
    lo_copy.wait()


def local(nctx, nhead, lq, lk, lv, ld, gain, sq, sk, sv, lens):
    hbm = pl.BlockSpec(memory_space=pl.ANY)
    vm = pl.BlockSpec(memory_space=pltpu.VMEM)
    dma = pltpu.SemaphoreType.DMA
    width = NH * T
    return pl.pallas_call(
        functools.partial(kernel, nctx, nhead),
        out_shape=(
            jax.ShapeDtypeStruct((T, width), BF16),
            jax.ShapeDtypeStruct((T, width), BF16),
        ),
        in_specs=[pl.BlockSpec(memory_space=pltpu.SMEM), hbm, hbm, hbm, vm, vm, hbm, hbm, hbm],
        out_specs=(hbm, hbm),
        scratch_shapes=[
            pltpu.VMEM((T, width), BF16),
            pltpu.VMEM((T, width), BF16),
            pltpu.VMEM((T, width), BF16),
            pltpu.VMEM((width, T), BF16),
            pltpu.VMEM(((BACK + 1) * 2 * T, T), BF16),
            pltpu.VMEM(((BACK + 1) * 2 * T, 2 * T), BF16),
            pltpu.VMEM((T, 9 * T), F32),
            pltpu.VMEM((NH, T), F32),
            pltpu.VMEM((NH, T), F32),
            pltpu.VMEM((NH, T), F32),
            pltpu.VMEM((NH, T), F32),
            pltpu.VMEM((NH, T, T), BF16),
            pltpu.VMEM((NH, T, T), BF16),
            pltpu.VMEM((LANE, T, T), F32),
            pltpu.VMEM((LANE, T, T), BF16),
            pltpu.VMEM((NH, T, T), BF16),
            pltpu.VMEM((LANE, T, T), BF16),
            pltpu.VMEM((LANE, T, T), BF16),
            pltpu.VMEM((NH, T, T), F32),
            pltpu.VMEM((NH, T, T), F32),
            pltpu.VMEM((8, T), F32),
            pltpu.VMEM((nhead, 8, T), F32),
            pltpu.VMEM((T, width), BF16),
            pltpu.VMEM((T, width), BF16),
            dma((5 + NH,)),
            dma((BACK, 2)),
            dma((BACK, 2)),
            dma((BACK + 1, 2)),
            dma((BACK + 1, 2)),
            dma((NH,)),
            dma((NH,)),
            dma(()),
            dma(()),
            dma((LANE,)),
            dma((LANE,)),
            dma((LANE,)),
            dma((LANE,)),
            dma((LANE,)),
            dma((LANE,)),
            dma((nhead,)),
            dma((nhead,)),
            dma((2,)),
        ],
        compiler_params=pltpu.CompilerParams(
            collective_id=0, has_side_effects=True, vmem_limit_bytes=40 * 2**20
        ),
    )(lens, lq, lk, lv, ld, gain.reshape(NH, T), sq, sk, sv)


def solution(mesh):
    placed = (
        P("ctx", "head"),
        P("ctx", "head"),
        P("ctx", "head"),
        P("head", "ctx"),
        P("head"),
        P("ctx", "head"),
        P("ctx", "head"),
        P("ctx", "head"),
        P(),
    )
    return jax.shard_map(
        functools.partial(local, mesh.shape["ctx"], mesh.shape["head"]),
        mesh=mesh,
        in_specs=placed,
        out_specs=(P("ctx", "head"), P("ctx", "head")),
        check_vma=False,
    )
```

```python
import functools
import math

import jax
import jax.numpy as jnp
from jax import lax
from jax.experimental import pallas as pl
from jax.experimental.pallas import tpu as pltpu
from jax.sharding import PartitionSpec as P

MESH = pl.DeviceIdType.MESH
F32 = jnp.float32
BF16 = jnp.bfloat16
LOG2E = 1.4426950408889634
T = 128
NH = 8
BACK = 4
NEG = -1e30


def nt(a, b, **kw):
    return lax.dot_general(a, b, (((1,), (1,)), ((), ())), preferred_element_type=F32, **kw)


def mm(a, b, **kw):
    return jnp.dot(a, b, preferred_element_type=F32, **kw)


def rcopy(src, dst, send, recv, dev):
    return pltpu.make_async_remote_copy(
        src_ref=src, dst_ref=dst, send_sem=send, recv_sem=recv, device_id=dev, device_id_type=MESH
    )


def kernel(
    nctx,
    nhead,
    lens_hbm,
    lq_hbm,
    lk_hbm,
    lv_hbm,
    ld_hbm,
    gain_hbm,
    sq_hbm,
    sk_hbm,
    sv_hbm,
    lout,
    sout,
    lq,
    lk,
    lv,
    qs,
    kbuf,
    vbuf,
    bias,
    fown,
    fsib,
    uown,
    usib,
    vst,
    y0,
    abuf,
    eg,
    mixed,
    squares,
    yloc,
    ybuf,
    lens,
    ld_ref,
    gain_ref,
    in_sem,
    k0_s,
    k0_r,
    kv_s,
    kv_r,
    ks_s,
    ks_r,
    u_s,
    u_r,
    f_s,
    f_r,
    a_s,
    a_r,
    e_s,
    e_r,
    yy_s,
    yy_r,
):
    c = lax.axis_index("ctx")
    hd = lax.axis_index("head")
    lane = lax.rem(c, 2)
    nxt = (lax.rem(c + 2, nctx), hd)
    prv = (lax.rem(c + nctx - 2, nctx), hd)
    sib = (c + 1 - 2 * lane, hd)
    first = c * T
    heads = range(NH)

    bar = pltpu.get_barrier_semaphore()
    pl.semaphore_signal(bar, inc=1, device_id=sib, device_id_type=MESH)

    @pl.when(lane == 1)
    def _():
        for dev in (nxt, prv):
            pl.semaphore_signal(bar, inc=1, device_id=dev, device_id_type=MESH)

    for i in range(1, nhead):
        pl.semaphore_signal(
            bar, inc=1, device_id=(c, lax.rem(hd + i, nhead)), device_id_type=MESH
        )

    def back(i):
        return pl.ds((BACK - i) * 2 * T, 2 * T)

    row_a, row_b = pl.ds(BACK * 2 * T, T), pl.ds((BACK * 2 + 1) * T, T)
    own = pl.ds(pl.multiple_of((BACK * 2 + lane) * T, T), T)
    vc = pl.ds(0, T)
    lens_in = pltpu.make_async_copy(lens_hbm, lens, in_sem.at[5 + NH])
    ld_in = pltpu.make_async_copy(ld_hbm, ld_ref, in_sem.at[6 + NH])
    gain_in = pltpu.make_async_copy(gain_hbm, gain_ref, in_sem.at[7 + NH])
    loads = [
        pltpu.make_async_copy(lk_hbm, lk, in_sem.at[0]),
        pltpu.make_async_copy(lv_hbm, lv, in_sem.at[1]),
        pltpu.make_async_copy(sk_hbm, kbuf.at[own], in_sem.at[2]),
        pltpu.make_async_copy(sv_hbm, vbuf.at[own, vc], in_sem.at[3]),
        pltpu.make_async_copy(lq_hbm, lq, in_sem.at[4]),
    ]
    for h in heads:
        loads.append(
            pltpu.make_async_copy(
                sq_hbm.at[:, pl.ds(h * T, T)], qs.at[pl.ds(h * T, T)], in_sem.at[5 + h]
            )
        )
    for cp in [lens_in, ld_in, *loads, gain_in]:
        cp.start()

    lens_in.wait()
    pos = first + lax.broadcasted_iota(jnp.int32, (8, T), 1)
    start = jnp.int32(0)
    low = jnp.zeros((8, T), jnp.int32)
    low_end = jnp.int32(0)
    for d in range(lens.shape[0]):
        low = jnp.where(pos >= start, start, low)
        low_end = jnp.where(first + T - 1 >= start, start, low_end)
        start = start + lens[d]
    rel_row = (low - first).astype(F32)
    rel_col = jnp.broadcast_to(rel_row[0:1], (T, T)).T
    row_f = lax.broadcasted_iota(jnp.int32, (T, T), 0).astype(F32)
    col_f = lax.broadcasted_iota(jnp.int32, (T, T), 1).astype(F32)

    ld_in.wait()
    tri = jnp.where(row_f <= col_f, 1.0, 0.0)
    both = jnp.concatenate([tri, jnp.ones((T, T), F32)], axis=1)
    sums = mm(ld_ref[...], both, precision=lax.Precision.HIGHEST)
    g = sums[:, :T]
    gend = sums[:, T:]
    key_scale = jnp.where(pos >= low_end, jnp.exp(gend - g), 0.0)
    fown[...] = jnp.where(low_end >= first, 0.0, jnp.exp(gend))

    f_copy = rcopy(fown, fsib, f_s, f_r, sib)

    def u_copy(h):
        return rcopy(uown.at[h], usib.at[h], u_s.at[h], u_r.at[h], sib)

    def e_copy(h):
        return rcopy(abuf.at[BACK - 1, h], abuf.at[BACK - 1, h], e_s.at[h], e_r.at[h], sib)

    def a_copy(i, h):
        src = y0.at[h] if i == 0 else abuf.at[i - 1, h]
        return rcopy(src, abuf.at[i, h], a_s.at[i, h], a_r.at[i, h], nxt)

    def pair(view, rows, to_rows, send, recv, dev):
        return [
            rcopy(kbuf.at[rows], kbuf.at[to_rows], send.at[view, 0], recv.at[view, 0], dev),
            rcopy(vbuf.at[rows, vc], vbuf.at[to_rows, vc], send.at[view, 1], recv.at[view, 1], dev),
        ]

    first_a, first_b = pl.ds((BACK - 1) * 2 * T, T), pl.ds((BACK * 2 - 1) * T, T)
    k_a = pair(0, row_a, row_a, ks_s, ks_r, sib)
    k0_a = pair(0, row_a, first_a, k0_s, k0_r, nxt)
    k0_b = pair(1, row_b, first_b, k0_s, k0_r, nxt)

    def kv_next(i):
        return pair(i - 1, back(i), back(i + 1), kv_s, kv_r, nxt)

    def kv_side(i):
        return pair(i, back(i), back(i), ks_s, ks_r, sib)

    def y_copy(i):
        return rcopy(yloc, ybuf.at[i], yy_s.at[i], yy_r.at[i], (c, lax.rem(hd + i, nhead)))

    def kv_step(i):
        for cp in k0_a + k0_b if i == 1 else kv_next(i - 1):
            cp.wait_recv()
        for cp in (kv_next(i) if i < BACK else []) + kv_side(i):
            cp.start()

    pl.semaphore_wait(bar, nhead + 2 * lane)

    def update(h):
        kt = lk[:, pl.ds(h * T, T)].astype(F32).T
        sk = (kt * key_scale[h : h + 1]).astype(BF16)
        return mm(sk, lv[:, pl.ds(h * T, T)])

    own_ok = (col_f >= rel_col) & (col_f <= row_f)
    carried = jnp.where(rel_col < 0.0, 1.0, 0.0)

    def inside(h):
        hs = pl.ds(h * T, T)
        grow = g[h : h + 1]
        gcol = jnp.broadcast_to(grow, (T, T)).T
        eg[h] = jnp.exp(gcol) * carried
        decay = jnp.exp(jnp.where(own_ok, gcol - grow, NEG))
        w = (nt(lq[:, hs], lk[:, hs]) * decay).astype(BF16)
        mixed[h] = mm(w, lv[:, hs])

    def carry(state):
        acc = jnp.zeros((T, T), F32)
        for h in heads:
            m = mixed[h] + mm(lq[:, pl.ds(h * T, T)], state(h)) * eg[h]
            mixed[h] = m
            acc = acc + m * m
        squares[...] = acc

    def masks():
        for j in range(9):
            rel = col_f + float((j - 8) * T)
            ok = rel >= rel_col
            if j == 8:
                ok = ok & (col_f <= row_f)
            bias[:, pl.ds(j * T, T)] = jnp.where(ok, 0.0, NEG)
        vbuf[:, pl.ds(T, T)] = jnp.ones((vbuf.shape[0], T), BF16)

    @pl.when(lane == 0)
    def _():
        f_copy.start()
        loads[2].wait()
        loads[3].wait()
        for cp in k_a:
            cp.start()
        loads[0].wait()
        loads[1].wait()
        for h in heads:
            uown[h] = update(h).astype(BF16)
            u_copy(h).start()
        loads[4].wait()
        for h in heads:
            inside(h)
        masks()

        def state(h):
            e_copy(h).wait_recv()
            return abuf[BACK - 1, h]

        carry(state)

    @pl.when(lane == 1)
    def _():
        loads[2].wait()
        loads[3].wait()
        for cp in k0_b:
            cp.start()
        loads[0].wait()
        loads[1].wait()
        for h in heads:
            vst[h] = update(h)
        f_copy.wait_recv()
        f_b = fown[...]
        f_a = fsib[...]
        f_ab = f_a * f_b
        for h in heads:
            u_copy(h).wait_recv()
            v = f_b[h : h + 1] * usib[h].astype(F32) + vst[h]
            vst[h] = v
            y0[h] = v.astype(BF16)
            a_copy(0, h).start()
        for cp in k_a:
            cp.wait_recv()
        for cp in k0_a:
            cp.start()
        loads[4].wait()

        def step(i):
            for h in heads:
                a_copy(i - 1, h).wait_recv()
                y = vst[h] + f_ab[h : h + 1] * abuf[i - 1, h].astype(F32)
                abuf[i - 1, h] = y.astype(BF16)
                a_copy(i, h).start()

        for h in range(0, NH // 2):
            inside(h)
        kv_step(1)
        step(1)
        for h in range(NH // 2, NH):
            inside(h)
        kv_step(2)
        step(2)
        masks()
        kv_step(3)
        step(3)
        kv_step(4)

        def state(h):
            a_copy(BACK - 1, h).wait_recv()
            e_copy(h).start()
            e = abuf[BACK - 1, h].astype(F32)
            return (f_a[h : h + 1] * e + usib[h].astype(F32)).astype(BF16)

        carry(state)

    part = nt(jnp.ones((8, T), F32), squares[...], precision=lax.Precision.HIGHEST)
    yloc[...] = part
    for i in range(1, nhead):
        y_copy(i).start()

    @pl.when(lane == 0)
    def _():
        for i in range(1, BACK + 1):
            for cp in kv_side(i):
                cp.wait_recv()

    for cp in loads[5:]:
        cp.wait()
    window = pl.ds(pl.multiple_of(lane * T, T), 9 * T)
    scale2 = LOG2E / math.sqrt(T)
    for h in heads:
        hs = pl.ds(h * T, T)
        s = nt(qs[hs, :], kbuf[window, :]) * scale2 + bias[...]
        p = jnp.exp2(s - jnp.max(s, axis=1, keepdims=True)).astype(BF16)
        o = mm(p, vbuf[window, :])
        sout[:, hs] = (o[:, :T] / o[:, T:]).astype(BF16)

    gain_in.wait()
    total = part
    for i in range(1, nhead):
        y_copy(i).wait_recv()
        total = total + ybuf[i]
    inv_row = lax.rsqrt(total * (1.0 / (nhead * NH * T)) + 1e-05)
    inv = jnp.broadcast_to(inv_row[0:1], (T, T)).T
    for h in heads:
        lout[:, pl.ds(h * T, T)] = (mixed[h] * inv * gain_ref[pl.ds(h, 1), :]).astype(BF16)

    @pl.when(lane == 0)
    def _():
        f_copy.wait_send()
        for cp in k_a:
            cp.wait_send()
        for h in heads:
            u_copy(h).wait_send()

    @pl.when(lane == 1)
    def _():
        for cp in k0_a + k0_b:
            cp.wait_send()
        for i in range(1, BACK + 1):
            for cp in (kv_next(i) if i < BACK else []) + kv_side(i):
                cp.wait_send()
        for h in heads:
            e_copy(h).wait_send()
            for i in range(BACK):
                a_copy(i, h).wait_send()

    for i in range(1, nhead):
        y_copy(i).wait_send()


def local(nctx, nhead, lq, lk, lv, ld, gain, sq, sk, sv, lens):
    hbm = pl.BlockSpec(memory_space=pltpu.HBM)
    vm = pl.BlockSpec(memory_space=pltpu.VMEM)
    dma = pltpu.SemaphoreType.DMA
    width = NH * T
    return pl.pallas_call(
        functools.partial(kernel, nctx, nhead),
        out_shape=(
            jax.ShapeDtypeStruct((T, width), BF16),
            jax.ShapeDtypeStruct((T, width), BF16),
        ),
        in_specs=[hbm] * 9,
        out_specs=(vm, vm),
        scratch_shapes=[
            pltpu.VMEM((T, width), BF16),
            pltpu.VMEM((T, width), BF16),
            pltpu.VMEM((T, width), BF16),
            pltpu.VMEM((width, T), BF16),
            pltpu.VMEM(((BACK + 1) * 2 * T, T), BF16),
            pltpu.VMEM(((BACK + 1) * 2 * T, 2 * T), BF16),
            pltpu.VMEM((T, 9 * T), F32),
            pltpu.VMEM((NH, T), F32),
            pltpu.VMEM((NH, T), F32),
            pltpu.VMEM((NH, T, T), BF16),
            pltpu.VMEM((NH, T, T), BF16),
            pltpu.VMEM((NH, T, T), F32),
            pltpu.VMEM((NH, T, T), BF16),
            pltpu.VMEM((BACK, NH, T, T), BF16),
            pltpu.VMEM((NH, T, T), F32),
            pltpu.VMEM((NH, T, T), F32),
            pltpu.VMEM((T, T), F32),
            pltpu.VMEM((8, T), F32),
            pltpu.VMEM((nhead, 8, T), F32),
            pltpu.SMEM(lens.shape, jnp.int32),
            pltpu.VMEM((NH, T), F32),
            pltpu.VMEM((NH, T), F32),
            dma((8 + NH,)),
            dma((2, 2)),
            dma((2, 2)),
            dma((BACK, 2)),
            dma((BACK, 2)),
            dma((BACK + 1, 2)),
            dma((BACK + 1, 2)),
            dma((NH,)),
            dma((NH,)),
            dma(()),
            dma(()),
            dma((BACK, NH)),
            dma((BACK, NH)),
            dma((NH,)),
            dma((NH,)),
            dma((nhead,)),
            dma((nhead,)),
        ],
        compiler_params=pltpu.CompilerParams(
            collective_id=0, has_side_effects=True, vmem_limit_bytes=60 * 2**20
        ),
    )(lens, lq, lk, lv, ld, gain.reshape(NH, T), sq, sk, sv)


def solution(mesh):
    placed = (
        P("ctx", "head"),
        P("ctx", "head"),
        P("ctx", "head"),
        P("head", "ctx"),
        P("head"),
        P("ctx", "head"),
        P("ctx", "head"),
        P("ctx", "head"),
        P(),
    )
    return jax.shard_map(
        functools.partial(local, mesh.shape["ctx"], mesh.shape["head"]),
        mesh=mesh,
        in_specs=placed,
        out_specs=(P("ctx", "head"), P("ctx", "head")),
        check_vma=False,
    )
```

```python
import functools
import math

import jax
import jax.numpy as jnp
from jax import lax
from jax.experimental import pallas as pl
from jax.experimental.pallas import tpu as pltpu
from jax.sharding import PartitionSpec as P

MESH = pl.DeviceIdType.MESH
F32 = jnp.float32
BF16 = jnp.bfloat16
LOG2E = 1.4426950408889634
T = 128
NH = 8
BACK = 4
AHEAD = (1, 2, 5)
NEG = -1e30


def nt(a, b, **kw):
    return lax.dot_general(a, b, (((1,), (1,)), ((), ())), preferred_element_type=F32, **kw)


def mm(a, b, **kw):
    return jnp.dot(a, b, preferred_element_type=F32, **kw)


def rcopy(src, dst, send, recv, dev):
    return pltpu.make_async_remote_copy(
        src_ref=src, dst_ref=dst, send_sem=send, recv_sem=recv, device_id=dev, device_id_type=MESH
    )


def kernel(
    nctx,
    nhead,
    lens_hbm,
    lq_hbm,
    lk_hbm,
    lv_hbm,
    ld_hbm,
    gain_hbm,
    sq_hbm,
    sk_hbm,
    sv_hbm,
    lout,
    sout,
    lq,
    lk,
    lv,
    qs,
    kbuf,
    vbuf,
    kvia,
    vvia,
    bias,
    fown,
    fsib,
    uown,
    usib,
    vst,
    y0,
    abuf,
    eg,
    mixed,
    squares,
    yloc,
    ybuf,
    lens,
    ld_ref,
    gain_ref,
    in_sem,
    k0_s,
    k0_r,
    kv_s,
    kv_r,
    ks_s,
    ks_r,
    u_s,
    u_r,
    f_s,
    f_r,
    a_s,
    a_r,
    e_s,
    e_r,
    yy_s,
    yy_r,
):
    c = lax.axis_index("ctx")
    hd = lax.axis_index("head")
    lane = lax.rem(c, 2)
    nxt = (lax.rem(c + 2, nctx), hd)
    prv = (lax.rem(c + nctx - 2, nctx), hd)

    def core_a(j):
        return (lax.rem(c - lane + 2 * j + nctx, nctx), hd)

    sib = (c + 1 - 2 * lane, hd)
    first = c * T
    heads = range(NH)

    bar = pltpu.get_barrier_semaphore()
    pl.semaphore_signal(bar, inc=1, device_id=sib, device_id_type=MESH)

    pl.semaphore_signal(bar, inc=1, device_id=prv, device_id_type=MESH)

    @pl.when(lane == 0)
    def _():
        pl.semaphore_signal(bar, inc=1, device_id=nxt, device_id_type=MESH)
        for j in AHEAD[1:]:
            pl.semaphore_signal(bar, inc=1, device_id=core_a(-j), device_id_type=MESH)
        for j in AHEAD:
            peer = (lax.rem(c + 1 - 2 * j + nctx, nctx), hd)
            pl.semaphore_signal(bar, inc=1, device_id=peer, device_id_type=MESH)

    for i in range(1, nhead):
        pl.semaphore_signal(
            bar, inc=1, device_id=(c, lax.rem(hd + i, nhead)), device_id_type=MESH
        )

    def back(i):
        return pl.ds((BACK - i) * 2 * T, 2 * T)

    row_a, row_b = pl.ds(BACK * 2 * T, T), pl.ds((BACK * 2 + 1) * T, T)
    own = pl.ds(pl.multiple_of((BACK * 2 + lane) * T, T), T)
    vc = pl.ds(0, T)
    lens_in = pltpu.make_async_copy(lens_hbm, lens, in_sem.at[5 + NH])
    ld_in = pltpu.make_async_copy(ld_hbm, ld_ref, in_sem.at[6 + NH])
    gain_in = pltpu.make_async_copy(gain_hbm, gain_ref, in_sem.at[7 + NH])
    loads = [
        pltpu.make_async_copy(lk_hbm, lk, in_sem.at[0]),
        pltpu.make_async_copy(lv_hbm, lv, in_sem.at[1]),
        pltpu.make_async_copy(sk_hbm, kbuf.at[own], in_sem.at[2]),
        pltpu.make_async_copy(sv_hbm, vbuf.at[own, vc], in_sem.at[3]),
        pltpu.make_async_copy(lq_hbm, lq, in_sem.at[4]),
    ]
    for h in heads:
        loads.append(
            pltpu.make_async_copy(
                sq_hbm.at[:, pl.ds(h * T, T)], qs.at[pl.ds(h * T, T)], in_sem.at[5 + h]
            )
        )
    for cp in [lens_in, ld_in, *loads, gain_in]:
        cp.start()

    lens_in.wait()
    pos = first + lax.broadcasted_iota(jnp.int32, (8, T), 1)
    start = jnp.int32(0)
    low = jnp.zeros((8, T), jnp.int32)
    low_end = jnp.int32(0)
    for d in range(lens.shape[0]):
        low = jnp.where(pos >= start, start, low)
        low_end = jnp.where(first + T - 1 >= start, start, low_end)
        start = start + lens[d]
    rel_row = (low - first).astype(F32)
    rel_col = jnp.broadcast_to(rel_row[0:1], (T, T)).T
    row_f = lax.broadcasted_iota(jnp.int32, (T, T), 0).astype(F32)
    col_f = lax.broadcasted_iota(jnp.int32, (T, T), 1).astype(F32)

    ld_in.wait()
    tri = jnp.where(row_f <= col_f, 1.0, 0.0)
    both = jnp.concatenate([tri, jnp.ones((T, T), F32)], axis=1)
    sums = mm(ld_ref[...], both, precision=lax.Precision.HIGHEST)
    g = sums[:, :T]
    gend = sums[:, T:]
    key_scale = jnp.where(pos >= low_end, jnp.exp(gend - g), 0.0)
    fown[...] = jnp.where(low_end >= first, 0.0, jnp.exp(gend))

    f_copy = rcopy(fown, fsib, f_s, f_r, sib)

    def u_copy(h):
        return rcopy(uown.at[h], usib.at[h], u_s.at[h], u_r.at[h], sib)

    def e_copy(h):
        return rcopy(abuf.at[BACK - 1, h], abuf.at[BACK - 1, h], e_s.at[h], e_r.at[h], sib)

    def a_copy(i, h):
        src = y0.at[h] if i == 0 else abuf.at[i - 1, h]
        return rcopy(src, abuf.at[i, h], a_s.at[i, h], a_r.at[i, h], nxt)

    def pair(view, rows, to_rows, send, recv, dev):
        return [
            rcopy(kbuf.at[rows], kbuf.at[to_rows], send.at[view, 0], recv.at[view, 0], dev),
            rcopy(vbuf.at[rows, vc], vbuf.at[to_rows, vc], send.at[view, 1], recv.at[view, 1], dev),
        ]

    k_b = pair(0, row_b, row_b, ks_s, ks_r, sib)
    k_a = pair(5, row_a, row_a, ks_s, ks_r, sib)

    def ahead(n, side):
        j = AHEAD[n]
        if j > BACK:
            to = pl.ds(pl.multiple_of(side * T, T), T)
            keys, values = kvia.at[to], vvia.at[to]
        else:
            to = pl.ds(pl.multiple_of(((BACK - j) * 2 + side) * T, T), T)
            keys, values = kbuf.at[to], vbuf.at[to, vc]
        dev = core_a(j)
        return [
            rcopy(kbuf.at[own], keys, k0_s.at[n, side, 0], k0_r.at[n, side, 0], dev),
            rcopy(vbuf.at[own, vc], values, k0_s.at[n, side, 1], k0_r.at[n, side, 1], dev),
        ]

    own_out = [cp for n in (2, 0, 1) for cp in ahead(n, lane)]
    kv_down4 = [
        rcopy(kvia, kbuf.at[back(4)], kv_s.at[1, 0], kv_r.at[1, 0], prv),
        rcopy(vvia, vbuf.at[back(4), vc], kv_s.at[1, 1], kv_r.at[1, 1], prv),
    ]
    kv_down3 = pair(0, back(4), back(3), kv_s, kv_r, prv)

    def kv_side(i):
        return pair(i, back(i), back(i), ks_s, ks_r, sib)

    def y_copy(i):
        return rcopy(yloc, ybuf.at[i], yy_s.at[i], yy_r.at[i], (c, lax.rem(hd + i, nhead)))

    def hand_on(arrivals, sends):
        for cp in arrivals:
            cp.wait_recv()
        for cp in sends:
            cp.start()

    def hand_in(sends):
        loads[2].wait()
        loads[3].wait()
        for cp in sends:
            cp.start()

    pl.semaphore_wait(bar, nhead + 4)

    def update(h):
        kt = lk[:, pl.ds(h * T, T)].astype(F32).T
        sk = (kt * key_scale[h : h + 1]).astype(BF16)
        return mm(sk, lv[:, pl.ds(h * T, T)])

    own_ok = (col_f >= rel_col) & (col_f <= row_f)
    carried = jnp.where(rel_col < 0.0, 1.0, 0.0)

    def inside(h):
        hs = pl.ds(h * T, T)
        grow = g[h : h + 1]
        gcol = jnp.broadcast_to(grow, (T, T)).T
        eg[h] = jnp.exp(gcol) * carried
        decay = jnp.exp(jnp.where(own_ok, gcol - grow, NEG))
        w = (nt(lq[:, hs], lk[:, hs]) * decay).astype(BF16)
        mixed[h] = mm(w, lv[:, hs])

    def carry(state):
        acc = jnp.zeros((T, T), F32)
        for h in heads:
            m = mixed[h] + mm(lq[:, pl.ds(h * T, T)], state(h)) * eg[h]
            mixed[h] = m
            acc = acc + m * m
        squares[...] = acc

    def masks():
        for j in range(9):
            rel = col_f + float((j - 8) * T)
            ok = rel >= rel_col
            if j == 8:
                ok = ok & (col_f <= row_f)
            bias[:, pl.ds(j * T, T)] = jnp.where(ok, 0.0, NEG)
        vbuf[:, pl.ds(T, T)] = jnp.ones((vbuf.shape[0], T), BF16)

    @pl.when(lane == 0)
    def _():
        f_copy.start()
        hand_in(own_out + k_a)
        loads[0].wait()
        loads[1].wait()
        for h in heads:
            uown[h] = update(h).astype(BF16)
            u_copy(h).start()
        loads[4].wait()
        for h in range(0, NH // 2):
            inside(h)
        hand_on(ahead(2, 0) + ahead(2, 1), kv_down4)
        for h in range(NH // 2, NH):
            inside(h)
        masks()
        hand_on(ahead(0, 0) + ahead(0, 1), kv_side(1))
        hand_on(ahead(1, 0) + ahead(1, 1), kv_side(2))
        hand_on(kv_down4, kv_down3 + kv_side(4))

        def state(h):
            e_copy(h).wait_recv()
            return abuf[BACK - 1, h]

        carry(state)

    @pl.when(lane == 1)
    def _():
        hand_in(own_out + k_b)
        loads[0].wait()
        loads[1].wait()
        for h in heads:
            vst[h] = update(h)
        f_copy.wait_recv()
        f_b = fown[...]
        f_a = fsib[...]
        f_ab = f_a * f_b
        for h in heads:
            u_copy(h).wait_recv()
            v = f_b[h : h + 1] * usib[h].astype(F32) + vst[h]
            vst[h] = v
            y0[h] = v.astype(BF16)
            a_copy(0, h).start()
        loads[4].wait()

        def step(i):
            for h in heads:
                a_copy(i - 1, h).wait_recv()
                y = vst[h] + f_ab[h : h + 1] * abuf[i - 1, h].astype(F32)
                abuf[i - 1, h] = y.astype(BF16)
                a_copy(i, h).start()

        for h in range(0, NH // 2):
            inside(h)
        step(1)
        for h in range(NH // 2, NH):
            inside(h)
        step(2)
        masks()
        step(3)

        def state(h):
            a_copy(BACK - 1, h).wait_recv()
            e_copy(h).start()
            e = abuf[BACK - 1, h].astype(F32)
            return (f_a[h : h + 1] * e + usib[h].astype(F32)).astype(BF16)

        carry(state)

    part = nt(jnp.ones((8, T), F32), squares[...], precision=lax.Precision.HIGHEST)
    yloc[...] = part
    for i in range(1, nhead):
        y_copy(i).start()

    @pl.when(lane == 0)
    def _():
        hand_on(kv_down3 + k_b, kv_side(3))

    @pl.when(lane == 1)
    def _():
        for cp in k_a:
            cp.wait_recv()
        for i in range(1, BACK + 1):
            for cp in kv_side(i):
                cp.wait_recv()

    for cp in loads[5:]:
        cp.wait()
    window = pl.ds(pl.multiple_of(lane * T, T), 9 * T)
    scale2 = LOG2E / math.sqrt(T)
    for h in heads:
        hs = pl.ds(h * T, T)
        s = nt(qs[hs, :], kbuf[window, :]) * scale2 + bias[...]
        p = jnp.exp2(s - jnp.max(s, axis=1, keepdims=True)).astype(BF16)
        o = mm(p, vbuf[window, :])
        sout[:, hs] = (o[:, :T] / o[:, T:]).astype(BF16)

    gain_in.wait()
    total = part
    for i in range(1, nhead):
        y_copy(i).wait_recv()
        total = total + ybuf[i]
    inv_row = lax.rsqrt(total * (1.0 / (nhead * NH * T)) + 1e-05)
    inv = jnp.broadcast_to(inv_row[0:1], (T, T)).T
    for h in heads:
        lout[:, pl.ds(h * T, T)] = (mixed[h] * inv * gain_ref[pl.ds(h, 1), :]).astype(BF16)

    @pl.when(lane == 0)
    def _():
        f_copy.wait_send()
        for cp in k_a + own_out + kv_down4 + kv_down3:
            cp.wait_send()
        for i in range(1, BACK + 1):
            for cp in kv_side(i):
                cp.wait_send()
        for h in heads:
            u_copy(h).wait_send()

    @pl.when(lane == 1)
    def _():
        for cp in k_b + own_out:
            cp.wait_send()
        for h in heads:
            e_copy(h).wait_send()
            for i in range(BACK):
                a_copy(i, h).wait_send()

    for i in range(1, nhead):
        y_copy(i).wait_send()


def local(nctx, nhead, lq, lk, lv, ld, gain, sq, sk, sv, lens):
    hbm = pl.BlockSpec(memory_space=pltpu.HBM)
    vm = pl.BlockSpec(memory_space=pltpu.VMEM)
    dma = pltpu.SemaphoreType.DMA
    width = NH * T
    return pl.pallas_call(
        functools.partial(kernel, nctx, nhead),
        out_shape=(
            pltpu.VMEM((T, width), BF16),
            pltpu.VMEM((T, width), BF16),
        ),
        in_specs=[hbm] * 9,
        out_specs=(vm, vm),
        scratch_shapes=[
            pltpu.VMEM((T, width), BF16),
            pltpu.VMEM((T, width), BF16),
            pltpu.VMEM((T, width), BF16),
            pltpu.VMEM((width, T), BF16),
            pltpu.VMEM(((BACK + 1) * 2 * T, T), BF16),
            pltpu.VMEM(((BACK + 1) * 2 * T, 2 * T), BF16),
            pltpu.VMEM((2 * T, T), BF16),
            pltpu.VMEM((2 * T, T), BF16),
            pltpu.VMEM((T, 9 * T), F32),
            pltpu.VMEM((NH, T), F32),
            pltpu.VMEM((NH, T), F32),
            pltpu.VMEM((NH, T, T), BF16),
            pltpu.VMEM((NH, T, T), BF16),
            pltpu.VMEM((NH, T, T), F32),
            pltpu.VMEM((NH, T, T), BF16),
            pltpu.VMEM((BACK, NH, T, T), BF16),
            pltpu.VMEM((NH, T, T), F32),
            pltpu.VMEM((NH, T, T), F32),
            pltpu.VMEM((T, T), F32),
            pltpu.VMEM((8, T), F32),
            pltpu.VMEM((nhead, 8, T), F32),
            pltpu.SMEM(lens.shape, jnp.int32),
            pltpu.VMEM((NH, T), F32),
            pltpu.VMEM((NH, T), F32),
            dma((8 + NH,)),
            dma((len(AHEAD), 2, 2)),
            dma((len(AHEAD), 2, 2)),
            dma((2, 2)),
            dma((2, 2)),
            dma((BACK + 2, 2)),
            dma((BACK + 2, 2)),
            dma((NH,)),
            dma((NH,)),
            dma(()),
            dma(()),
            dma((BACK, NH)),
            dma((BACK, NH)),
            dma((NH,)),
            dma((NH,)),
            dma((nhead,)),
            dma((nhead,)),
        ],
        compiler_params=pltpu.CompilerParams(
            collective_id=0, has_side_effects=True, vmem_limit_bytes=60 * 2**20
        ),
    )(lens, lq, lk, lv, ld, gain.reshape(NH, T), sq, sk, sv)


def solution(mesh):
    placed = (
        P("ctx", "head"),
        P("ctx", "head"),
        P("ctx", "head"),
        P("head", "ctx"),
        P("head"),
        P("ctx", "head"),
        P("ctx", "head"),
        P("ctx", "head"),
        P(),
    )
    return jax.shard_map(
        functools.partial(local, mesh.shape["ctx"], mesh.shape["head"]),
        mesh=mesh,
        in_specs=placed,
        out_specs=(P("ctx", "head"), P("ctx", "head")),
        check_vma=False,
    )
```

```python
import functools
import math

import jax
import jax.numpy as jnp
from jax import lax
from jax.experimental import pallas as pl
from jax.experimental.pallas import tpu as pltpu
from jax.sharding import PartitionSpec as P

MESH = pl.DeviceIdType.MESH
F32 = jnp.float32
BF16 = jnp.bfloat16
LOG2E = 1.4426950408889634
T = 128
NH = 8
BACK = 4
AHEAD = (1, 2, 5)
NEG = -1e30


def nt(a, b, **kw):
    return lax.dot_general(a, b, (((1,), (1,)), ((), ())), preferred_element_type=F32, **kw)


def mm(a, b, **kw):
    return jnp.dot(a, b, preferred_element_type=F32, **kw)


def rcopy(src, dst, send, recv, dev):
    return pltpu.make_async_remote_copy(
        src_ref=src, dst_ref=dst, send_sem=send, recv_sem=recv, device_id=dev, device_id_type=MESH
    )


def kernel(
    nctx,
    nhead,
    lens_hbm,
    lq_hbm,
    lk_hbm,
    lv_hbm,
    ld_hbm,
    gain_hbm,
    sq_hbm,
    sk_hbm,
    sv_hbm,
    lout,
    sout,
    lq,
    lk,
    lv,
    qs,
    kbuf,
    vbuf,
    kvia,
    vvia,
    bias,
    fown,
    fsib,
    uown,
    usib,
    vst,
    y0,
    abuf,
    eg,
    mixed,
    squares,
    yloc,
    ybuf,
    lens,
    ld_ref,
    gain_ref,
    in_sem,
    k0_s,
    k0_r,
    kv_s,
    kv_r,
    ks_s,
    ks_r,
    u_s,
    u_r,
    f_s,
    f_r,
    a_s,
    a_r,
    e_s,
    e_r,
    yy_s,
    yy_r,
):
    c = lax.axis_index("ctx")
    hd = lax.axis_index("head")
    lane = lax.rem(c, 2)
    nxt = (lax.rem(c + 2, nctx), hd)
    prv = (lax.rem(c + nctx - 2, nctx), hd)

    def core_a(j):
        return (lax.rem(c - lane + 2 * j + nctx, nctx), hd)

    sib = (c + 1 - 2 * lane, hd)
    first = c * T
    heads = range(NH)

    bar = pltpu.get_barrier_semaphore()
    pl.semaphore_signal(bar, inc=1, device_id=sib, device_id_type=MESH)

    pl.semaphore_signal(bar, inc=1, device_id=prv, device_id_type=MESH)

    @pl.when(lane == 0)
    def _():
        pl.semaphore_signal(bar, inc=1, device_id=nxt, device_id_type=MESH)
        for j in AHEAD[1:]:
            pl.semaphore_signal(bar, inc=1, device_id=core_a(-j), device_id_type=MESH)
        for j in AHEAD:
            peer = (lax.rem(c + 1 - 2 * j + nctx, nctx), hd)
            pl.semaphore_signal(bar, inc=1, device_id=peer, device_id_type=MESH)

    for i in range(1, nhead):
        pl.semaphore_signal(
            bar, inc=1, device_id=(c, lax.rem(hd + i, nhead)), device_id_type=MESH
        )

    def back(i):
        return pl.ds((BACK - i) * 2 * T, 2 * T)

    row_a, row_b = pl.ds(BACK * 2 * T, T), pl.ds((BACK * 2 + 1) * T, T)
    own = pl.ds(pl.multiple_of((BACK * 2 + lane) * T, T), T)
    vc = pl.ds(0, T)
    lens_in = pltpu.make_async_copy(lens_hbm, lens, in_sem.at[5 + NH])
    ld_in = pltpu.make_async_copy(ld_hbm, ld_ref, in_sem.at[6 + NH])
    gain_in = pltpu.make_async_copy(gain_hbm, gain_ref, in_sem.at[7 + NH])
    loads = [
        pltpu.make_async_copy(lk_hbm, lk, in_sem.at[0]),
        pltpu.make_async_copy(lv_hbm, lv, in_sem.at[1]),
        pltpu.make_async_copy(sk_hbm, kbuf.at[own], in_sem.at[2]),
        pltpu.make_async_copy(sv_hbm, vbuf.at[own, vc], in_sem.at[3]),
        pltpu.make_async_copy(lq_hbm, lq, in_sem.at[4]),
    ]
    for h in heads:
        loads.append(
            pltpu.make_async_copy(
                sq_hbm.at[:, pl.ds(h * T, T)], qs.at[pl.ds(h * T, T)], in_sem.at[5 + h]
            )
        )
    for cp in [lens_in, ld_in, *loads, gain_in]:
        cp.start()

    lens_in.wait()
    pos = first + lax.broadcasted_iota(jnp.int32, (8, T), 1)
    start = jnp.int32(0)
    low = jnp.zeros((8, T), jnp.int32)
    low_end = jnp.int32(0)
    for d in range(lens.shape[0]):
        low = jnp.where(pos >= start, start, low)
        low_end = jnp.where(first + T - 1 >= start, start, low_end)
        start = start + lens[d]
    rel_row = (low - first).astype(F32)
    rel_col = jnp.broadcast_to(rel_row[0:1], (T, T)).T
    row_f = lax.broadcasted_iota(jnp.int32, (T, T), 0).astype(F32)
    col_f = lax.broadcasted_iota(jnp.int32, (T, T), 1).astype(F32)

    ld_in.wait()
    tri = jnp.where(row_f <= col_f, 1.0, 0.0)
    both = jnp.concatenate([tri, jnp.ones((T, T), F32)], axis=1)
    sums = mm(ld_ref[...], both, precision=lax.Precision.HIGHEST)
    g = sums[:, :T]
    gend = sums[:, T:]
    key_scale = jnp.where(pos >= low_end, jnp.exp(gend - g), 0.0)
    fown[...] = jnp.where(low_end >= first, 0.0, jnp.exp(gend))

    f_copy = rcopy(fown, fsib, f_s, f_r, sib)

    def u_copy(h):
        return rcopy(uown.at[h], usib.at[h], u_s.at[h], u_r.at[h], sib)

    def e_copy(h):
        return rcopy(abuf.at[BACK - 1, h], abuf.at[BACK - 1, h], e_s.at[h], e_r.at[h], sib)

    def a_copy(i, h):
        src = y0.at[h] if i == 0 else abuf.at[i - 1, h]
        return rcopy(src, abuf.at[i, h], a_s.at[i, h], a_r.at[i, h], nxt)

    def send(i, h):
        @pl.when(c + 2 < nctx)
        def _():
            a_copy(i, h).start()

    def arrive(i, h):
        @pl.when(c >= 2)
        def _():
            a_copy(i, h).wait_recv()

        @pl.when(c < 2)
        def _():
            abuf[i, h] = jnp.zeros((T, T), BF16)

    def pair(view, rows, to_rows, send, recv, dev):
        return [
            rcopy(kbuf.at[rows], kbuf.at[to_rows], send.at[view, 0], recv.at[view, 0], dev),
            rcopy(vbuf.at[rows, vc], vbuf.at[to_rows, vc], send.at[view, 1], recv.at[view, 1], dev),
        ]

    k_b = pair(0, row_b, row_b, ks_s, ks_r, sib)
    k_a = pair(5, row_a, row_a, ks_s, ks_r, sib)

    def ahead(n, side):
        j = AHEAD[n]
        if j > BACK:
            to = pl.ds(pl.multiple_of(side * T, T), T)
            keys, values = kvia.at[to], vvia.at[to]
        else:
            to = pl.ds(pl.multiple_of(((BACK - j) * 2 + side) * T, T), T)
            keys, values = kbuf.at[to], vbuf.at[to, vc]
        dev = core_a(j)
        return [
            rcopy(kbuf.at[own], keys, k0_s.at[n, side, 0], k0_r.at[n, side, 0], dev),
            rcopy(vbuf.at[own, vc], values, k0_s.at[n, side, 1], k0_r.at[n, side, 1], dev),
        ]

    own_out = [cp for n in (2, 0, 1) for cp in ahead(n, lane)]
    kv_down4 = [
        rcopy(kvia, kbuf.at[back(4)], kv_s.at[1, 0], kv_r.at[1, 0], prv),
        rcopy(vvia, vbuf.at[back(4), vc], kv_s.at[1, 1], kv_r.at[1, 1], prv),
    ]
    kv_down3 = pair(0, back(4), back(3), kv_s, kv_r, prv)

    def kv_side(i):
        return pair(i, back(i), back(i), ks_s, ks_r, sib)

    def y_copy(i):
        return rcopy(yloc, ybuf.at[i], yy_s.at[i], yy_r.at[i], (c, lax.rem(hd + i, nhead)))

    def hand_on(arrivals, sends, side=()):
        for cp in arrivals:
            cp.wait_recv()
        for cp in sends:
            cp.start()

        @pl.when(c >= 2)
        def _():
            for cp in side:
                cp.start()

    def hand_in(sends):
        loads[2].wait()
        loads[3].wait()
        for cp in sends:
            cp.start()

    pl.semaphore_wait(bar, nhead + 4)

    def update(h):
        kt = lk[:, pl.ds(h * T, T)].astype(F32).T
        sk = (kt * key_scale[h : h + 1]).astype(BF16)
        return mm(sk, lv[:, pl.ds(h * T, T)])

    own_ok = (col_f >= rel_col) & (col_f <= row_f)
    carried = jnp.where(rel_col < 0.0, 1.0, 0.0)

    def inside(h):
        hs = pl.ds(h * T, T)
        grow = g[h : h + 1]
        gcol = jnp.broadcast_to(grow, (T, T)).T
        eg[h] = jnp.exp(gcol) * carried
        decay = jnp.exp(jnp.where(own_ok, gcol - grow, NEG))
        w = (nt(lq[:, hs], lk[:, hs]) * decay).astype(BF16)
        mixed[h] = mm(w, lv[:, hs])

    def carry(state):
        acc = jnp.zeros((T, T), F32)
        for h in heads:
            m = mixed[h] + mm(lq[:, pl.ds(h * T, T)], state(h)) * eg[h]
            mixed[h] = m
            acc = acc + m * m
        squares[...] = acc

    def masks():
        for j in range(9):
            rel = col_f + float((j - 8) * T)
            ok = rel >= rel_col
            if j == 8:
                ok = ok & (col_f <= row_f)
            bias[:, pl.ds(j * T, T)] = jnp.where(ok, 0.0, NEG)
        vbuf[:, pl.ds(T, T)] = jnp.ones((vbuf.shape[0], T), BF16)

    @pl.when(lane == 0)
    def _():
        f_copy.start()
        hand_in(own_out + k_a)
        loads[0].wait()
        loads[1].wait()
        for h in heads:
            uown[h] = update(h).astype(BF16)
            u_copy(h).start()
        loads[4].wait()
        for h in range(0, NH // 2):
            inside(h)
        hand_on(ahead(2, 0) + ahead(2, 1), kv_down4)
        for h in range(NH // 2, NH):
            inside(h)
        masks()
        hand_on(ahead(0, 0) + ahead(0, 1), [], kv_side(1))
        hand_on(ahead(1, 0) + ahead(1, 1), [], kv_side(2))
        hand_on(kv_down4, kv_down3, kv_side(4))

        def state(h):
            e_copy(h).wait_recv()
            return abuf[BACK - 1, h]

        carry(state)

    @pl.when(lane == 1)
    def _():
        hand_in(own_out + k_b)
        loads[0].wait()
        loads[1].wait()
        for h in heads:
            vst[h] = update(h)
        f_copy.wait_recv()
        f_b = fown[...]
        f_a = fsib[...]
        f_ab = f_a * f_b
        for h in heads:
            u_copy(h).wait_recv()
            v = f_b[h : h + 1] * usib[h].astype(F32) + vst[h]
            vst[h] = v
            y0[h] = v.astype(BF16)
            send(0, h)
        loads[4].wait()

        def step(i):
            for h in heads:
                arrive(i - 1, h)
                y = vst[h] + f_ab[h : h + 1] * abuf[i - 1, h].astype(F32)
                abuf[i - 1, h] = y.astype(BF16)
                send(i, h)

        for h in range(0, NH // 2):
            inside(h)
        step(1)
        for h in range(NH // 2, NH):
            inside(h)
        step(2)
        masks()
        step(3)

        def state(h):
            arrive(BACK - 1, h)
            e_copy(h).start()
            e = abuf[BACK - 1, h].astype(F32)
            return (f_a[h : h + 1] * e + usib[h].astype(F32)).astype(BF16)

        carry(state)

    part = nt(jnp.ones((8, T), F32), squares[...], precision=lax.Precision.HIGHEST)
    yloc[...] = part
    for i in range(1, nhead):
        y_copy(i).start()

    @pl.when(lane == 0)
    def _():
        hand_on(kv_down3 + k_b, [], kv_side(3))

    @pl.when(lane == 1)
    def _():
        for cp in k_a:
            cp.wait_recv()

        @pl.when(c >= 2)
        def _():
            for i in range(1, BACK + 1):
                for cp in kv_side(i):
                    cp.wait_recv()

        @pl.when(c < 2)
        def _():
            kbuf[pl.ds(0, BACK * 2 * T), :] = jnp.zeros((BACK * 2 * T, T), BF16)
            vbuf[pl.ds(0, BACK * 2 * T), vc] = jnp.zeros((BACK * 2 * T, T), BF16)

    for cp in loads[5:]:
        cp.wait()
    window = pl.ds(pl.multiple_of(lane * T, T), 9 * T)
    scale2 = LOG2E / math.sqrt(T)
    for h in heads:
        hs = pl.ds(h * T, T)
        s = nt(qs[hs, :], kbuf[window, :]) * scale2 + bias[...]
        p = jnp.exp2(s - jnp.max(s, axis=1, keepdims=True)).astype(BF16)
        o = mm(p, vbuf[window, :])
        sout[:, hs] = (o[:, :T] / o[:, T:]).astype(BF16)

    gain_in.wait()
    total = part
    for i in range(1, nhead):
        y_copy(i).wait_recv()
        total = total + ybuf[i]
    inv_row = lax.rsqrt(total * (1.0 / (nhead * NH * T)) + 1e-05)
    inv = jnp.broadcast_to(inv_row[0:1], (T, T)).T
    for h in heads:
        lout[:, pl.ds(h * T, T)] = (mixed[h] * inv * gain_ref[pl.ds(h, 1), :]).astype(BF16)

    @pl.when(lane == 0)
    def _():
        f_copy.wait_send()
        for cp in k_a + own_out + kv_down4 + kv_down3:
            cp.wait_send()

        @pl.when(c >= 2)
        def _():
            for i in range(1, BACK + 1):
                for cp in kv_side(i):
                    cp.wait_send()

        for h in heads:
            u_copy(h).wait_send()

    @pl.when(lane == 1)
    def _():
        for cp in k_b + own_out:
            cp.wait_send()
        for h in heads:
            e_copy(h).wait_send()

        @pl.when(c + 2 < nctx)
        def _():
            for h in heads:
                for i in range(BACK):
                    a_copy(i, h).wait_send()

    for i in range(1, nhead):
        y_copy(i).wait_send()


def local(nctx, nhead, lq, lk, lv, ld, gain, sq, sk, sv, lens):
    hbm = pl.BlockSpec(memory_space=pltpu.HBM)
    vm = pl.BlockSpec(memory_space=pltpu.VMEM)
    dma = pltpu.SemaphoreType.DMA
    width = NH * T
    return pl.pallas_call(
        functools.partial(kernel, nctx, nhead),
        out_shape=(
            pltpu.VMEM((T, width), BF16),
            pltpu.VMEM((T, width), BF16),
        ),
        in_specs=[hbm] * 9,
        out_specs=(vm, vm),
        scratch_shapes=[
            pltpu.VMEM((T, width), BF16),
            pltpu.VMEM((T, width), BF16),
            pltpu.VMEM((T, width), BF16),
            pltpu.VMEM((width, T), BF16),
            pltpu.VMEM(((BACK + 1) * 2 * T, T), BF16),
            pltpu.VMEM(((BACK + 1) * 2 * T, 2 * T), BF16),
            pltpu.VMEM((2 * T, T), BF16),
            pltpu.VMEM((2 * T, T), BF16),
            pltpu.VMEM((T, 9 * T), F32),
            pltpu.VMEM((NH, T), F32),
            pltpu.VMEM((NH, T), F32),
            pltpu.VMEM((NH, T, T), BF16),
            pltpu.VMEM((NH, T, T), BF16),
            pltpu.VMEM((NH, T, T), F32),
            pltpu.VMEM((NH, T, T), BF16),
            pltpu.VMEM((BACK, NH, T, T), BF16),
            pltpu.VMEM((NH, T, T), F32),
            pltpu.VMEM((NH, T, T), F32),
            pltpu.VMEM((T, T), F32),
            pltpu.VMEM((8, T), F32),
            pltpu.VMEM((nhead, 8, T), F32),
            pltpu.SMEM(lens.shape, jnp.int32),
            pltpu.VMEM((NH, T), F32),
            pltpu.VMEM((NH, T), F32),
            dma((8 + NH,)),
            dma((len(AHEAD), 2, 2)),
            dma((len(AHEAD), 2, 2)),
            dma((2, 2)),
            dma((2, 2)),
            dma((BACK + 2, 2)),
            dma((BACK + 2, 2)),
            dma((NH,)),
            dma((NH,)),
            dma(()),
            dma(()),
            dma((BACK, NH)),
            dma((BACK, NH)),
            dma((NH,)),
            dma((NH,)),
            dma((nhead,)),
            dma((nhead,)),
        ],
        compiler_params=pltpu.CompilerParams(
            collective_id=0, has_side_effects=True, vmem_limit_bytes=60 * 2**20
        ),
    )(lens, lq, lk, lv, ld, gain.reshape(NH, T), sq, sk, sv)


def solution(mesh):
    placed = (
        P("ctx", "head"),
        P("ctx", "head"),
        P("ctx", "head"),
        P("head", "ctx"),
        P("head"),
        P("ctx", "head"),
        P("ctx", "head"),
        P("ctx", "head"),
        P(),
    )
    return jax.shard_map(
        functools.partial(local, mesh.shape["ctx"], mesh.shape["head"]),
        mesh=mesh,
        in_specs=placed,
        out_specs=(P("ctx", "head"), P("ctx", "head")),
        check_vma=False,
    )
```

```python
import functools
import math

import jax
import jax.numpy as jnp
from jax import lax
from jax.experimental import pallas as pl
from jax.experimental.pallas import tpu as pltpu
from jax.sharding import PartitionSpec as P

MESH = pl.DeviceIdType.MESH
F32 = jnp.float32
BF16 = jnp.bfloat16
LOG2E = 1.4426950408889634
T = 128
NH = 8
BACK = 4
AHEAD = (1, 5)
NEG = -1e30


def nt(a, b, **kw):
    return lax.dot_general(a, b, (((1,), (1,)), ((), ())), preferred_element_type=F32, **kw)


def mm(a, b, **kw):
    return jnp.dot(a, b, preferred_element_type=F32, **kw)


def rcopy(src, dst, send, recv, dev):
    return pltpu.make_async_remote_copy(
        src_ref=src, dst_ref=dst, send_sem=send, recv_sem=recv, device_id=dev, device_id_type=MESH
    )


def kernel(
    nctx,
    nhead,
    lens_hbm,
    lq_hbm,
    lk_hbm,
    lv_hbm,
    ld_hbm,
    gain_hbm,
    sq_hbm,
    sk_hbm,
    sv_hbm,
    lout,
    sout,
    lq,
    lk,
    lv,
    qs,
    kbuf,
    vbuf,
    kvia,
    vvia,
    bias,
    fown,
    fsib,
    uown,
    usib,
    vst,
    y0,
    abuf,
    eg,
    mixed,
    squares,
    yloc,
    ybuf,
    lens,
    ld_ref,
    gain_ref,
    in_sem,
    k0_s,
    k0_r,
    kv_s,
    kv_r,
    ks_s,
    ks_r,
    u_s,
    u_r,
    f_s,
    f_r,
    a_s,
    a_r,
    e_s,
    e_r,
    yy_s,
    yy_r,
):
    c = lax.axis_index("ctx")
    hd = lax.axis_index("head")
    lane = lax.rem(c, 2)
    nxt = (lax.rem(c + 2, nctx), hd)
    prv = (lax.rem(c + nctx - 2, nctx), hd)

    def core_a(j):
        return (lax.rem(c - lane + 2 * j + nctx, nctx), hd)

    sib = (c + 1 - 2 * lane, hd)
    first = c * T
    heads = range(NH)

    bar = pltpu.get_barrier_semaphore()
    pl.semaphore_signal(bar, inc=1, device_id=sib, device_id_type=MESH)

    pl.semaphore_signal(bar, inc=1, device_id=prv, device_id_type=MESH)

    @pl.when(lane == 0)
    def _():
        pl.semaphore_signal(bar, inc=1, device_id=nxt, device_id_type=MESH)
        for j in AHEAD[1:]:
            pl.semaphore_signal(bar, inc=1, device_id=core_a(-j), device_id_type=MESH)
        for j in AHEAD:
            peer = (lax.rem(c + 1 - 2 * j + nctx, nctx), hd)
            pl.semaphore_signal(bar, inc=1, device_id=peer, device_id_type=MESH)

    for i in range(1, nhead):
        pl.semaphore_signal(
            bar, inc=1, device_id=(c, lax.rem(hd + i, nhead)), device_id_type=MESH
        )

    def back(i):
        return pl.ds((BACK - i) * 2 * T, 2 * T)

    row_a, row_b = pl.ds(BACK * 2 * T, T), pl.ds((BACK * 2 + 1) * T, T)
    own = pl.ds(pl.multiple_of((BACK * 2 + lane) * T, T), T)
    vc = pl.ds(0, T)
    lens_in = pltpu.make_async_copy(lens_hbm, lens, in_sem.at[5 + NH])
    ld_in = pltpu.make_async_copy(ld_hbm, ld_ref, in_sem.at[6 + NH])
    gain_in = pltpu.make_async_copy(gain_hbm, gain_ref, in_sem.at[7 + NH])
    loads = [
        pltpu.make_async_copy(lk_hbm, lk, in_sem.at[0]),
        pltpu.make_async_copy(lv_hbm, lv, in_sem.at[1]),
        pltpu.make_async_copy(sk_hbm, kbuf.at[own], in_sem.at[2]),
        pltpu.make_async_copy(sv_hbm, vbuf.at[own, vc], in_sem.at[3]),
        pltpu.make_async_copy(lq_hbm, lq, in_sem.at[4]),
    ]
    for h in heads:
        loads.append(
            pltpu.make_async_copy(
                sq_hbm.at[:, pl.ds(h * T, T)], qs.at[pl.ds(h * T, T)], in_sem.at[5 + h]
            )
        )
    for cp in [lens_in, ld_in, *loads[:4]]:
        cp.start()

    lens_in.wait()
    pos = first + lax.broadcasted_iota(jnp.int32, (8, T), 1)
    start = jnp.int32(0)
    low = jnp.zeros((8, T), jnp.int32)
    low_end = jnp.int32(0)
    for d in range(lens.shape[0]):
        low = jnp.where(pos >= start, start, low)
        low_end = jnp.where(first + T - 1 >= start, start, low_end)
        start = start + lens[d]
    rel_row = (low - first).astype(F32)
    rel_col = jnp.broadcast_to(rel_row[0:1], (T, T)).T
    row_f = lax.broadcasted_iota(jnp.int32, (T, T), 0).astype(F32)
    col_f = lax.broadcasted_iota(jnp.int32, (T, T), 1).astype(F32)

    ld_in.wait()
    tri = jnp.where(row_f <= col_f, 1.0, 0.0)
    both = jnp.concatenate([tri, jnp.ones((T, T), F32)], axis=1)
    sums = mm(ld_ref[...], both, precision=lax.Precision.HIGHEST)
    g = sums[:, :T]
    gend = sums[:, T:]
    key_scale = jnp.where(pos >= low_end, jnp.exp(gend - g), 0.0)
    fown[...] = jnp.where(low_end >= first, 0.0, jnp.exp(gend))

    f_copy = rcopy(fown, fsib, f_s, f_r, sib)

    def u_copy(h):
        return rcopy(uown.at[h], usib.at[h], u_s.at[h], u_r.at[h], sib)

    def e_copy(h):
        return rcopy(abuf.at[BACK - 1, h], abuf.at[BACK - 1, h], e_s.at[h], e_r.at[h], sib)

    def a_copy(i, h):
        src = y0.at[h] if i == 0 else abuf.at[i - 1, h]
        return rcopy(src, abuf.at[i, h], a_s.at[i, h], a_r.at[i, h], nxt)

    def send(i, h):
        @pl.when(c + 2 < nctx)
        def _():
            a_copy(i, h).start()

    def arrive(i, h):
        @pl.when(c >= 2)
        def _():
            a_copy(i, h).wait_recv()

        @pl.when(c < 2)
        def _():
            abuf[i, h] = jnp.zeros((T, T), BF16)

    def pair(view, rows, to_rows, send, recv, dev):
        return [
            rcopy(kbuf.at[rows], kbuf.at[to_rows], send.at[view, 0], recv.at[view, 0], dev),
            rcopy(vbuf.at[rows, vc], vbuf.at[to_rows, vc], send.at[view, 1], recv.at[view, 1], dev),
        ]

    k_b = pair(0, row_b, row_b, ks_s, ks_r, sib)
    k_a = pair(5, row_a, row_a, ks_s, ks_r, sib)

    def ahead(n, side):
        j = AHEAD[n]
        if j > BACK:
            to = pl.ds(pl.multiple_of(side * T, T), T)
            keys, values = kvia.at[to], vvia.at[to]
        else:
            to = pl.ds(pl.multiple_of(((BACK - j) * 2 + side) * T, T), T)
            keys, values = kbuf.at[to], vbuf.at[to, vc]
        dev = core_a(j)
        return [
            rcopy(kbuf.at[own], keys, k0_s.at[n, side, 0], k0_r.at[n, side, 0], dev),
            rcopy(vbuf.at[own, vc], values, k0_s.at[n, side, 1], k0_r.at[n, side, 1], dev),
        ]

    own_out = [cp for n in (1, 0) for cp in ahead(n, lane)]
    kv_down4 = [
        rcopy(kvia, kbuf.at[back(4)], kv_s.at[1, 0], kv_r.at[1, 0], prv),
        rcopy(vvia, vbuf.at[back(4), vc], kv_s.at[1, 1], kv_r.at[1, 1], prv),
    ]
    kv_down3 = pair(0, back(4), back(3), kv_s, kv_r, prv)
    kv_down2 = pair(2, back(3), back(2), kv_s, kv_r, prv)

    def kv_side(i):
        return pair(i, back(i), back(i), ks_s, ks_r, sib)

    def y_copy(i):
        return rcopy(yloc, ybuf.at[i], yy_s.at[i], yy_r.at[i], (c, lax.rem(hd + i, nhead)))

    def hand_on(arrivals, sends, side=()):
        for cp in arrivals:
            cp.wait_recv()
        for cp in sends:
            cp.start()

        @pl.when(c >= 2)
        def _():
            for cp in side:
                cp.start()

    def hand_in(sends):
        loads[2].wait()
        loads[3].wait()
        for cp in sends:
            cp.start()

    def later():
        for cp in [*loads[4:], gain_in]:
            cp.start()

    pl.semaphore_wait(bar, nhead + 3)

    def update(h):
        kt = lk[:, pl.ds(h * T, T)].astype(F32).T
        sk = (kt * key_scale[h : h + 1]).astype(BF16)
        return mm(sk, lv[:, pl.ds(h * T, T)])

    own_ok = (col_f >= rel_col) & (col_f <= row_f)
    carried = jnp.where(rel_col < 0.0, 1.0, 0.0)

    def inside(h):
        hs = pl.ds(h * T, T)
        grow = g[h : h + 1]
        gcol = jnp.broadcast_to(grow, (T, T)).T
        eg[h] = jnp.exp(gcol) * carried
        decay = jnp.exp(jnp.where(own_ok, gcol - grow, NEG))
        w = (nt(lq[:, hs], lk[:, hs]) * decay).astype(BF16)
        mixed[h] = mm(w, lv[:, hs])

    def carry(state):
        acc = jnp.zeros((T, T), F32)
        for h in heads:
            m = mixed[h] + mm(lq[:, pl.ds(h * T, T)], state(h)) * eg[h]
            mixed[h] = m
            acc = acc + m * m
        squares[...] = acc

    def masks():
        for j in range(9):
            rel = col_f + float((j - 8) * T)
            ok = rel >= rel_col
            if j == 8:
                ok = ok & (col_f <= row_f)
            bias[:, pl.ds(j * T, T)] = jnp.where(ok, 0.0, NEG)
        vbuf[:, pl.ds(T, T)] = jnp.ones((vbuf.shape[0], T), BF16)

    @pl.when(lane == 0)
    def _():
        f_copy.start()
        hand_in(own_out + k_a)
        loads[0].wait()
        loads[1].wait()
        for h in heads:
            uown[h] = update(h).astype(BF16)
            u_copy(h).start()
            if h == 3:
                later()
        loads[4].wait()
        for h in range(0, NH // 2):
            inside(h)
        hand_on(ahead(1, 0) + ahead(1, 1), kv_down4)
        for h in range(NH // 2, NH):
            inside(h)
        masks()
        hand_on(ahead(0, 0) + ahead(0, 1), [], kv_side(1))
        hand_on(kv_down4, kv_down3, kv_side(4))
        hand_on(kv_down3, kv_down2, kv_side(3))

        def state(h):
            e_copy(h).wait_recv()
            return abuf[BACK - 1, h]

        carry(state)

    @pl.when(lane == 1)
    def _():
        hand_in(own_out + k_b)
        loads[0].wait()
        loads[1].wait()
        for h in heads:
            vst[h] = update(h)
            if h == 3:
                later()
        f_copy.wait_recv()
        f_b = fown[...]
        f_a = fsib[...]
        f_ab = f_a * f_b
        for h in heads:
            u_copy(h).wait_recv()
            v = f_b[h : h + 1] * usib[h].astype(F32) + vst[h]
            vst[h] = v
            y0[h] = v.astype(BF16)
            send(0, h)
        loads[4].wait()

        def step(i):
            for h in heads:
                arrive(i - 1, h)
                y = vst[h] + f_ab[h : h + 1] * abuf[i - 1, h].astype(F32)
                abuf[i - 1, h] = y.astype(BF16)
                send(i, h)

        for h in range(0, NH // 2):
            inside(h)
        step(1)
        for h in range(NH // 2, NH):
            inside(h)
        step(2)
        masks()
        step(3)

        def state(h):
            arrive(BACK - 1, h)
            e_copy(h).start()
            e = abuf[BACK - 1, h].astype(F32)
            return (f_a[h : h + 1] * e + usib[h].astype(F32)).astype(BF16)

        carry(state)

    part = nt(jnp.ones((8, T), F32), squares[...], precision=lax.Precision.HIGHEST)
    yloc[...] = part
    for i in sorted(range(1, nhead), key=lambda i: -min(i, nhead - i)):
        y_copy(i).start()

    @pl.when(lane == 0)
    def _():
        hand_on(kv_down2 + k_b, [], kv_side(2))

    @pl.when(lane == 1)
    def _():
        for cp in k_a:
            cp.wait_recv()

        @pl.when(c >= 2)
        def _():
            for i in range(1, BACK + 1):
                for cp in kv_side(i):
                    cp.wait_recv()

        @pl.when(c < 2)
        def _():
            kbuf[pl.ds(0, BACK * 2 * T), :] = jnp.zeros((BACK * 2 * T, T), BF16)
            vbuf[pl.ds(0, BACK * 2 * T), vc] = jnp.zeros((BACK * 2 * T, T), BF16)

    for cp in loads[5:]:
        cp.wait()
    window = pl.ds(pl.multiple_of(lane * T, T), 9 * T)
    scale2 = LOG2E / math.sqrt(T)
    for h in heads:
        hs = pl.ds(h * T, T)
        s = nt(qs[hs, :], kbuf[window, :]) * scale2 + bias[...]
        p = jnp.exp2(s - jnp.max(s, axis=1, keepdims=True)).astype(BF16)
        o = mm(p, vbuf[window, :])
        sout[:, hs] = (o[:, :T] / o[:, T:]).astype(BF16)

    @pl.when(lane == 0)
    def _():
        f_copy.wait_send()
        for cp in k_a + own_out + kv_down4 + kv_down3 + kv_down2:
            cp.wait_send()

        @pl.when(c >= 2)
        def _():
            for i in range(1, BACK + 1):
                for cp in kv_side(i):
                    cp.wait_send()

        for h in heads:
            u_copy(h).wait_send()

    @pl.when(lane == 1)
    def _():
        for cp in k_b + own_out:
            cp.wait_send()
        for h in heads:
            e_copy(h).wait_send()

        @pl.when(c + 2 < nctx)
        def _():
            for h in heads:
                for i in range(BACK):
                    a_copy(i, h).wait_send()

    gain_in.wait()
    total = part
    for i in range(1, nhead):
        y_copy(i).wait_recv()
        total = total + ybuf[i]
    inv_row = lax.rsqrt(total * (1.0 / (nhead * NH * T)) + 1e-05)
    inv = jnp.broadcast_to(inv_row[0:1], (T, T)).T
    for h in heads:
        lout[:, pl.ds(h * T, T)] = (mixed[h] * inv * gain_ref[pl.ds(h, 1), :]).astype(BF16)

    for i in range(1, nhead):
        y_copy(i).wait_send()


def local(nctx, nhead, lq, lk, lv, ld, gain, sq, sk, sv, lens):
    hbm = pl.BlockSpec(memory_space=pltpu.HBM)
    vm = pl.BlockSpec(memory_space=pltpu.VMEM)
    dma = pltpu.SemaphoreType.DMA
    width = NH * T
    return pl.pallas_call(
        functools.partial(kernel, nctx, nhead),
        out_shape=(
            pltpu.VMEM((T, width), BF16),
            pltpu.VMEM((T, width), BF16),
        ),
        in_specs=[hbm] * 9,
        out_specs=(vm, vm),
        scratch_shapes=[
            pltpu.VMEM((T, width), BF16),
            pltpu.VMEM((T, width), BF16),
            pltpu.VMEM((T, width), BF16),
            pltpu.VMEM((width, T), BF16),
            pltpu.VMEM(((BACK + 1) * 2 * T, T), BF16),
            pltpu.VMEM(((BACK + 1) * 2 * T, 2 * T), BF16),
            pltpu.VMEM((2 * T, T), BF16),
            pltpu.VMEM((2 * T, T), BF16),
            pltpu.VMEM((T, 9 * T), F32),
            pltpu.VMEM((NH, T), F32),
            pltpu.VMEM((NH, T), F32),
            pltpu.VMEM((NH, T, T), BF16),
            pltpu.VMEM((NH, T, T), BF16),
            pltpu.VMEM((NH, T, T), F32),
            pltpu.VMEM((NH, T, T), BF16),
            pltpu.VMEM((BACK, NH, T, T), BF16),
            pltpu.VMEM((NH, T, T), F32),
            pltpu.VMEM((NH, T, T), F32),
            pltpu.VMEM((T, T), F32),
            pltpu.VMEM((8, T), F32),
            pltpu.VMEM((nhead, 8, T), F32),
            pltpu.SMEM(lens.shape, jnp.int32),
            pltpu.VMEM((NH, T), F32),
            pltpu.VMEM((NH, T), F32),
            dma((8 + NH,)),
            dma((len(AHEAD), 2, 2)),
            dma((len(AHEAD), 2, 2)),
            dma((3, 2)),
            dma((3, 2)),
            dma((BACK + 2, 2)),
            dma((BACK + 2, 2)),
            dma((NH,)),
            dma((NH,)),
            dma(()),
            dma(()),
            dma((BACK, NH)),
            dma((BACK, NH)),
            dma((NH,)),
            dma((NH,)),
            dma((nhead,)),
            dma((nhead,)),
        ],
        compiler_params=pltpu.CompilerParams(
            collective_id=0, has_side_effects=True, vmem_limit_bytes=60 * 2**20
        ),
    )(lens, lq, lk, lv, ld, gain.reshape(NH, T), sq, sk, sv)


def solution(mesh):
    placed = (
        P("ctx", "head"),
        P("ctx", "head"),
        P("ctx", "head"),
        P("head", "ctx"),
        P("head"),
        P("ctx", "head"),
        P("ctx", "head"),
        P("ctx", "head"),
        P(),
    )
    return jax.shard_map(
        functools.partial(local, mesh.shape["ctx"], mesh.shape["head"]),
        mesh=mesh,
        in_specs=placed,
        out_specs=(P("ctx", "head"), P("ctx", "head")),
        check_vma=False,
    )
```

```python
import functools
import math

import jax
import jax.numpy as jnp
from jax import lax
from jax.experimental import pallas as pl
from jax.experimental.pallas import tpu as pltpu
from jax.sharding import PartitionSpec as P

MESH = pl.DeviceIdType.MESH
F32 = jnp.float32
BF16 = jnp.bfloat16
LOG2E = 1.4426950408889634
T = 128
NH = 8
BACK = 4
AHEAD = (1, 5)
NEG = -1e30


def nt(a, b, **kw):
    return lax.dot_general(a, b, (((1,), (1,)), ((), ())), preferred_element_type=F32, **kw)


def mm(a, b, **kw):
    return jnp.dot(a, b, preferred_element_type=F32, **kw)


def rcopy(src, dst, send, recv, dev):
    return pltpu.make_async_remote_copy(
        src_ref=src, dst_ref=dst, send_sem=send, recv_sem=recv, device_id=dev, device_id_type=MESH
    )


def kernel(
    nctx,
    nhead,
    lens_hbm,
    lq_hbm,
    lk_hbm,
    lv_hbm,
    ld_hbm,
    gain_hbm,
    sq_hbm,
    sk_hbm,
    sv_hbm,
    lout,
    sout,
    lq,
    lk,
    lv,
    qs,
    kbuf,
    vbuf,
    kvia,
    vvia,
    bias,
    fown,
    fsib,
    uown,
    usib,
    vst,
    y0,
    abuf,
    eg,
    mixed,
    squares,
    yloc,
    ybuf,
    lens,
    ld_ref,
    gain_ref,
    in_sem,
    k0_s,
    k0_r,
    kv_s,
    kv_r,
    ks_s,
    ks_r,
    u_s,
    u_r,
    f_s,
    f_r,
    a_s,
    a_r,
    e_s,
    e_r,
    yy_s,
    yy_r,
):
    c = lax.axis_index("ctx")
    hd = lax.axis_index("head")
    lane = lax.rem(c, 2)
    nxt = (lax.rem(c + 2, nctx), hd)
    prv = (lax.rem(c + nctx - 2, nctx), hd)

    def core_a(j):
        return (lax.rem(c - lane + 2 * j + nctx, nctx), hd)

    sib = (c + 1 - 2 * lane, hd)
    first = c * T
    heads = range(NH)

    bar = pltpu.get_barrier_semaphore()
    pl.semaphore_signal(bar, inc=1, device_id=sib, device_id_type=MESH)

    pl.semaphore_signal(bar, inc=1, device_id=prv, device_id_type=MESH)

    @pl.when(lane == 0)
    def _():
        pl.semaphore_signal(bar, inc=1, device_id=nxt, device_id_type=MESH)
        for j in AHEAD[1:]:
            pl.semaphore_signal(bar, inc=1, device_id=core_a(-j), device_id_type=MESH)
        for j in AHEAD:
            peer = (lax.rem(c + 1 - 2 * j + nctx, nctx), hd)
            pl.semaphore_signal(bar, inc=1, device_id=peer, device_id_type=MESH)

    for i in range(1, nhead):
        pl.semaphore_signal(
            bar, inc=1, device_id=(c, lax.rem(hd + i, nhead)), device_id_type=MESH
        )

    def back(i):
        return pl.ds((BACK - i) * 2 * T, 2 * T)

    row_a, row_b = pl.ds(BACK * 2 * T, T), pl.ds((BACK * 2 + 1) * T, T)
    own = pl.ds(pl.multiple_of((BACK * 2 + lane) * T, T), T)
    vc = pl.ds(0, T)
    lens_in = pltpu.make_async_copy(lens_hbm, lens, in_sem.at[5 + NH])
    ld_in = pltpu.make_async_copy(ld_hbm, ld_ref, in_sem.at[6 + NH])
    gain_in = pltpu.make_async_copy(gain_hbm, gain_ref, in_sem.at[7 + NH])
    loads = [
        pltpu.make_async_copy(lk_hbm, lk, in_sem.at[0]),
        pltpu.make_async_copy(lv_hbm, lv, in_sem.at[1]),
        pltpu.make_async_copy(sk_hbm, kbuf.at[own], in_sem.at[2]),
        pltpu.make_async_copy(sv_hbm, vbuf.at[own, vc], in_sem.at[3]),
        pltpu.make_async_copy(lq_hbm, lq, in_sem.at[4]),
    ]
    for h in heads:
        loads.append(
            pltpu.make_async_copy(
                sq_hbm.at[:, pl.ds(h * T, T)], qs.at[pl.ds(h * T, T)], in_sem.at[5 + h]
            )
        )
    for cp in [lens_in, ld_in, *loads[:4]]:
        cp.start()

    lens_in.wait()
    pos = first + lax.broadcasted_iota(jnp.int32, (8, T), 1)
    start = jnp.int32(0)
    low = jnp.zeros((8, T), jnp.int32)
    low_end = jnp.int32(0)
    for d in range(lens.shape[0]):
        low = jnp.where(pos >= start, start, low)
        low_end = jnp.where(first + T - 1 >= start, start, low_end)
        start = start + lens[d]
    rel_row = (low - first).astype(F32)
    rel_col = jnp.broadcast_to(rel_row[0:1], (T, T)).T
    row_f = lax.broadcasted_iota(jnp.int32, (T, T), 0).astype(F32)
    col_f = lax.broadcasted_iota(jnp.int32, (T, T), 1).astype(F32)

    ld_in.wait()
    tri = jnp.where(row_f <= col_f, 1.0, 0.0)
    both = jnp.concatenate([tri, jnp.ones((T, T), F32)], axis=1)
    sums = mm(ld_ref[...], both, precision=lax.Precision.HIGHEST)
    g = sums[:, :T]
    gend = sums[:, T:]
    key_scale = jnp.where(pos >= low_end, jnp.exp(gend - g), 0.0)
    fown[...] = jnp.where(low_end >= first, 0.0, jnp.exp(gend))

    f_copy = rcopy(fown, fsib, f_s, f_r, sib)

    def u_copy(h):
        return rcopy(uown.at[h], usib.at[h], u_s.at[h], u_r.at[h], sib)

    def e_copy(h):
        return rcopy(abuf.at[BACK - 1, h], abuf.at[BACK - 1, h], e_s.at[h], e_r.at[h], sib)

    def a_copy(i, h):
        src = y0.at[h] if i == 0 else abuf.at[i - 1, h]
        return rcopy(src, abuf.at[i, h], a_s.at[i, h], a_r.at[i, h], nxt)

    def send(i, h):
        @pl.when(c + 2 < nctx)
        def _():
            a_copy(i, h).start()

    def arrive(i, h):
        @pl.when(c >= 2)
        def _():
            a_copy(i, h).wait_recv()

        @pl.when(c < 2)
        def _():
            abuf[i, h] = jnp.zeros((T, T), BF16)

    def pair(view, rows, to_rows, send, recv, dev):
        return [
            rcopy(kbuf.at[rows], kbuf.at[to_rows], send.at[view, 0], recv.at[view, 0], dev),
            rcopy(vbuf.at[rows, vc], vbuf.at[to_rows, vc], send.at[view, 1], recv.at[view, 1], dev),
        ]

    k_b = pair(0, row_b, row_b, ks_s, ks_r, sib)
    k_a = pair(5, row_a, row_a, ks_s, ks_r, sib)

    def ahead(n, side):
        j = AHEAD[n]
        if j > BACK:
            to = pl.ds(pl.multiple_of(side * T, T), T)
            keys, values = kvia.at[to], vvia.at[to]
        else:
            to = pl.ds(pl.multiple_of(((BACK - j) * 2 + side) * T, T), T)
            keys, values = kbuf.at[to], vbuf.at[to, vc]
        dev = core_a(j)
        return [
            rcopy(kbuf.at[own], keys, k0_s.at[n, side, 0], k0_r.at[n, side, 0], dev),
            rcopy(vbuf.at[own, vc], values, k0_s.at[n, side, 1], k0_r.at[n, side, 1], dev),
        ]

    own_out = [cp for n in (1, 0) for cp in ahead(n, lane)]
    kv_down4 = [
        rcopy(kvia, kbuf.at[back(4)], kv_s.at[1, 0], kv_r.at[1, 0], prv),
        rcopy(vvia, vbuf.at[back(4), vc], kv_s.at[1, 1], kv_r.at[1, 1], prv),
    ]
    kv_down3 = pair(0, back(4), back(3), kv_s, kv_r, prv)
    kv_down2 = pair(2, back(3), back(2), kv_s, kv_r, prv)

    def kv_side(i):
        return pair(i, back(i), back(i), ks_s, ks_r, sib)

    def y_copy(i):
        return rcopy(yloc, ybuf.at[i], yy_s.at[i], yy_r.at[i], (c, lax.rem(hd + i, nhead)))

    def hand_on(arrivals, sends, side=()):
        for cp in arrivals:
            cp.wait_recv()
        for cp in sends:
            cp.start()

        @pl.when(c >= 2)
        def _():
            for cp in side:
                cp.start()

    def hand_in(sends):
        loads[2].wait()
        loads[3].wait()
        for cp in sends:
            cp.start()

    def later():
        for cp in [*loads[4:], gain_in]:
            cp.start()

    pl.semaphore_wait(bar, nhead + 3)

    def update(h):
        kt = lk[:, pl.ds(h * T, T)].astype(F32).T
        sk = (kt * key_scale[h : h + 1]).astype(BF16)
        return mm(sk, lv[:, pl.ds(h * T, T)])

    own_ok = (col_f >= rel_col) & (col_f <= row_f)
    carried = jnp.where(rel_col < 0.0, 1.0, 0.0)

    def inside(h):
        hs = pl.ds(h * T, T)
        grow = g[h : h + 1]
        gcol = jnp.broadcast_to(grow, (T, T)).T
        eg[h] = jnp.exp(gcol) * carried
        decay = jnp.exp(jnp.where(own_ok, gcol - grow, NEG))
        w = (nt(lq[:, hs], lk[:, hs]) * decay).astype(BF16)
        mixed[h] = mm(w, lv[:, hs])

    def carry(state):
        acc = jnp.zeros((T, T), F32)
        for h in heads:
            m = mixed[h] + mm(lq[:, pl.ds(h * T, T)], state(h)) * eg[h]
            mixed[h] = m
            acc = acc + m * m
        squares[...] = acc

    def masks():
        for j in range(9):
            rel = col_f + float((j - 8) * T)
            ok = rel >= rel_col
            if j == 8:
                ok = ok & (col_f <= row_f)
            bias[:, pl.ds(j * T, T)] = jnp.where(ok, 0.0, NEG)
        vbuf[:, pl.ds(T, T)] = jnp.ones((vbuf.shape[0], T), BF16)

    @pl.when(lane == 0)
    def _():
        f_copy.start()
        loads[0].wait()
        loads[1].wait()
        for h in heads:
            uown[h] = update(h).astype(BF16)
            u_copy(h).start()
            if h == 1:
                hand_in(own_out + k_a)
            if h == 3:
                later()
        loads[4].wait()
        for h in range(0, NH // 2):
            inside(h)
        hand_on(ahead(1, 0) + ahead(1, 1), kv_down4)
        for h in range(NH // 2, NH):
            inside(h)
        masks()
        hand_on(ahead(0, 0) + ahead(0, 1), [], kv_side(1))
        hand_on(kv_down4, kv_down3, kv_side(4))
        hand_on(kv_down3, kv_down2, kv_side(3))

        def state(h):
            e_copy(h).wait_recv()
            return abuf[BACK - 1, h]

        carry(state)

    @pl.when(lane == 1)
    def _():
        hand_in(own_out + k_b)
        loads[0].wait()
        loads[1].wait()
        for h in heads:
            vst[h] = update(h)
            if h == 3:
                later()
        f_copy.wait_recv()
        f_b = fown[...]
        f_a = fsib[...]
        f_ab = f_a * f_b
        for h in heads:
            u_copy(h).wait_recv()
            v = f_b[h : h + 1] * usib[h].astype(F32) + vst[h]
            vst[h] = v
            y0[h] = v.astype(BF16)
            send(0, h)
        loads[4].wait()

        def step(i):
            for h in heads:
                arrive(i - 1, h)
                y = vst[h] + f_ab[h : h + 1] * abuf[i - 1, h].astype(F32)
                abuf[i - 1, h] = y.astype(BF16)
                send(i, h)

        for h in range(0, NH // 2):
            inside(h)
        step(1)
        for h in range(NH // 2, NH):
            inside(h)
        step(2)
        masks()
        step(3)

        def state(h):
            arrive(BACK - 1, h)
            e_copy(h).start()
            e = abuf[BACK - 1, h].astype(F32)
            return (f_a[h : h + 1] * e + usib[h].astype(F32)).astype(BF16)

        carry(state)

    part = nt(jnp.ones((8, T), F32), squares[...], precision=lax.Precision.HIGHEST)
    yloc[...] = part
    for i in sorted(range(1, nhead), key=lambda i: -min(i, nhead - i)):
        y_copy(i).start()

    @pl.when(lane == 0)
    def _():
        hand_on(kv_down2 + k_b, [], kv_side(2))

    @pl.when(lane == 1)
    def _():
        for cp in k_a:
            cp.wait_recv()

        @pl.when(c >= 2)
        def _():
            for i in range(1, BACK + 1):
                for cp in kv_side(i):
                    cp.wait_recv()

        @pl.when(c < 2)
        def _():
            kbuf[pl.ds(0, BACK * 2 * T), :] = jnp.zeros((BACK * 2 * T, T), BF16)
            vbuf[pl.ds(0, BACK * 2 * T), vc] = jnp.zeros((BACK * 2 * T, T), BF16)

    for cp in loads[5:]:
        cp.wait()
    window = pl.ds(pl.multiple_of(lane * T, T), 9 * T)
    scale2 = LOG2E / math.sqrt(T)
    for h in heads:
        hs = pl.ds(h * T, T)
        s = nt(qs[hs, :], kbuf[window, :]) * scale2 + bias[...]
        p = jnp.exp2(s - jnp.max(s, axis=1, keepdims=True)).astype(BF16)
        o = mm(p, vbuf[window, :])
        sout[:, hs] = (o[:, :T] / o[:, T:]).astype(BF16)

    @pl.when(lane == 0)
    def _():
        f_copy.wait_send()
        for cp in k_a + own_out + kv_down4 + kv_down3 + kv_down2:
            cp.wait_send()

        @pl.when(c >= 2)
        def _():
            for i in range(1, BACK + 1):
                for cp in kv_side(i):
                    cp.wait_send()

        for h in heads:
            u_copy(h).wait_send()

    @pl.when(lane == 1)
    def _():
        for cp in k_b + own_out:
            cp.wait_send()
        for h in heads:
            e_copy(h).wait_send()

        @pl.when(c + 2 < nctx)
        def _():
            for h in heads:
                for i in range(BACK):
                    a_copy(i, h).wait_send()

    gain_in.wait()
    total = part
    for i in range(1, nhead):
        y_copy(i).wait_recv()
        total = total + ybuf[i]
    inv_row = lax.rsqrt(total * (1.0 / (nhead * NH * T)) + 1e-05)
    inv = jnp.broadcast_to(inv_row[0:1], (T, T)).T
    for h in heads:
        lout[:, pl.ds(h * T, T)] = (mixed[h] * inv * gain_ref[pl.ds(h, 1), :]).astype(BF16)

    for i in range(1, nhead):
        y_copy(i).wait_send()


def local(nctx, nhead, lq, lk, lv, ld, gain, sq, sk, sv, lens):
    hbm = pl.BlockSpec(memory_space=pltpu.HBM)
    vm = pl.BlockSpec(memory_space=pltpu.VMEM)
    dma = pltpu.SemaphoreType.DMA
    width = NH * T
    return pl.pallas_call(
        functools.partial(kernel, nctx, nhead),
        out_shape=(
            pltpu.VMEM((T, width), BF16),
            pltpu.VMEM((T, width), BF16),
        ),
        in_specs=[hbm] * 9,
        out_specs=(vm, vm),
        scratch_shapes=[
            pltpu.VMEM((T, width), BF16),
            pltpu.VMEM((T, width), BF16),
            pltpu.VMEM((T, width), BF16),
            pltpu.VMEM((width, T), BF16),
            pltpu.VMEM(((BACK + 1) * 2 * T, T), BF16),
            pltpu.VMEM(((BACK + 1) * 2 * T, 2 * T), BF16),
            pltpu.VMEM((2 * T, T), BF16),
            pltpu.VMEM((2 * T, T), BF16),
            pltpu.VMEM((T, 9 * T), F32),
            pltpu.VMEM((NH, T), F32),
            pltpu.VMEM((NH, T), F32),
            pltpu.VMEM((NH, T, T), BF16),
            pltpu.VMEM((NH, T, T), BF16),
            pltpu.VMEM((NH, T, T), F32),
            pltpu.VMEM((NH, T, T), BF16),
            pltpu.VMEM((BACK, NH, T, T), BF16),
            pltpu.VMEM((NH, T, T), F32),
            pltpu.VMEM((NH, T, T), F32),
            pltpu.VMEM((T, T), F32),
            pltpu.VMEM((8, T), F32),
            pltpu.VMEM((nhead, 8, T), F32),
            pltpu.SMEM(lens.shape, jnp.int32),
            pltpu.VMEM((NH, T), F32),
            pltpu.VMEM((NH, T), F32),
            dma((8 + NH,)),
            dma((len(AHEAD), 2, 2)),
            dma((len(AHEAD), 2, 2)),
            dma((3, 2)),
            dma((3, 2)),
            dma((BACK + 2, 2)),
            dma((BACK + 2, 2)),
            dma((NH,)),
            dma((NH,)),
            dma(()),
            dma(()),
            dma((BACK, NH)),
            dma((BACK, NH)),
            dma((NH,)),
            dma((NH,)),
            dma((nhead,)),
            dma((nhead,)),
        ],
        compiler_params=pltpu.CompilerParams(
            collective_id=0, has_side_effects=True, vmem_limit_bytes=60 * 2**20
        ),
    )(lens, lq, lk, lv, ld, gain.reshape(NH, T), sq, sk, sv)


def solution(mesh):
    placed = (
        P("ctx", "head"),
        P("ctx", "head"),
        P("ctx", "head"),
        P("head", "ctx"),
        P("head"),
        P("ctx", "head"),
        P("ctx", "head"),
        P("ctx", "head"),
        P(),
    )
    return jax.shard_map(
        functools.partial(local, mesh.shape["ctx"], mesh.shape["head"]),
        mesh=mesh,
        in_specs=placed,
        out_specs=(P("ctx", "head"), P("ctx", "head")),
        check_vma=False,
    )
```
